128 devices in a mesh: dp: 16 (over y, z), ctx: 8 (over x, core).
Axes of the slice: x: 4, y: 4, z: 4, core: 2. Of those that a mesh axis runs over, the one named last changes fastest.
Arguments:
- state_input: bfloat16 [32768, 4096], P(('dp', 'ctx')), may hold values from -6 to 6
- gate_values: bfloat16 [32768, 4096], P(('dp', 'ctx')), may hold values from -6 to 6
- input_matrix: bfloat16 [32768, 512], P(('dp', 'ctx')), may hold values from -1.2 to 1.2
- readout_matrix: bfloat16 [32768, 512], P(('dp', 'ctx')), may hold values from -1.1953125 to 1.1953125
- step_unbiased: float32 [32768, 64], P(('dp', 'ctx')), may hold values from -3 to 2560
- step_bias: float32 [64], replicated, may hold values from -1 to 0.5
- decay_rate_log: float32 [64], replicated
- skip_coefficients: float32 [64], replicated, may hold values from 3 to 10
- norm_gain: float32 [4096], replicated, may hold values from 0.1 to 8
- adapter_down: bfloat16 [64, 4096], replicated, may hold values from -0.09375 to 0.09375
- adapter_up: bfloat16 [64, 2048], replicated, may hold values from -0.75 to 0.75
- projection_weight: bfloat16 [2048, 4096], P(('dp', 'ctx')), may hold values from -0.09375 to 0.09375
- output_cotangent: bfloat16 [32768, 2048], P(('dp', 'ctx')), may hold values from -30 to 30
Outputs:
- input_gradient: bfloat16 [32768, 4096], P(('dp', 'ctx'))
- adapter_down_gradient: float32 [64, 4096], P(None, ('dp', 'ctx'))
- adapter_up_gradient: float32 [64, 2048], P(None, ('dp', 'ctx'))
The draws below stay inside these ranges and needn't reach their ends.
All inputs are finite; a program needn't handle non-finite values.
Results may differ from the reference program's by a relative error of at most 0.009.
Values may be sent and summed in bfloat16 or wider, within the bound.
A program may use at most 192 MiB of HBM per device.

```python
import math
import jax
import jax.numpy as jnp
from jax import lax

H = 64
P_SIZE = 64
N = 128
G = 4
OUTPUT_FEATURES = 2048
ADAPTER_RANK = 64
Q = 256
INNER_CHANNELS = 4096
SEQUENCE_LENGTH = 2048
TOTAL_ROWS = 32768
N_DP = 16


def spike_mask(key):
    spike_picks = jax.random.randint(jax.random.fold_in(key, 101), (N_DP, 2), 0, SEQUENCE_LENGTH)
    location_list = jnp.arange(SEQUENCE_LENGTH, dtype=jnp.int32)
    spike_hits = jnp.any(location_list[None, :, None] == spike_picks[:, None, :], axis=2)
    return spike_hits.reshape(N_DP * SEQUENCE_LENGTH)


def draw_step_unbiased(key, part):
    spike_hits = spike_mask(key)
    frozen_values = jnp.clip(0.8 * jax.random.normal(jax.random.fold_in(key, 1), (TOTAL_ROWS, H), jnp.float32), -3.0, 3.0)
    return jnp.where(spike_hits[:, None], jnp.float32(1.25 * SEQUENCE_LENGTH), frozen_values)


def draw_input_matrix(key, part):
    spike_hits = spike_mask(key)
    raw_values = jnp.clip(0.3 * jax.random.normal(jax.random.fold_in(key, 2), (TOTAL_ROWS, G * N), jnp.float32), -1.1875, 1.1875)
    clip_factor = jnp.where(spike_hits, jnp.float32(1.0 / (1.25 * SEQUENCE_LENGTH)), jnp.float32(1.0))
    return (raw_values * clip_factor[:, None]).astype(jnp.bfloat16)


def draw_decay_rate_log(key, part):
    head_ranks = jax.random.permutation(jax.random.fold_in(key, 3), H)
    rank_share = head_ranks.astype(jnp.float32) / H
    rate_pick = jax.random.uniform(jax.random.fold_in(key, 4), (H,), jnp.float32)
    slow_rates = jnp.exp(math.log(0.18) + rate_pick * (math.log(0.55) - math.log(0.18))) / SEQUENCE_LENGTH
    middle = jnp.exp(math.log(1.0 / 256) + rate_pick * (math.log(1.0 / 64) - math.log(1.0 / 256)))
    fast_rates = 1.0 / 45 + rate_pick * (1.0 / 22 - 1.0 / 45)
    head_rates = jnp.where(rank_share < 0.5, slow_rates, jnp.where(rank_share < 0.75, middle, fast_rates))
    return jnp.log(head_rates).astype(jnp.float32)


def draw_norm_gain(key, part):
    column_ramp = 0.5 + 1.5 * jnp.arange(INNER_CHANNELS, dtype=jnp.float32) / INNER_CHANNELS
    spread = jnp.exp(jax.random.uniform(jax.random.fold_in(key, 5), (INNER_CHANNELS,), jnp.float32, math.log(0.3), math.log(3.0)))
    return (column_ramp * spread).astype(jnp.float32)


def draw_output_cotangent(key, part):
    column_ramp = 0.5 + 1.5 * jnp.arange(OUTPUT_FEATURES, dtype=jnp.float32) / OUTPUT_FEATURES
    column_scale = column_ramp * jnp.exp(jax.random.uniform(jax.random.fold_in(key, 6), (OUTPUT_FEATURES,), jnp.float32, math.log(0.4), math.log(2.5)))
    body_values = jnp.clip(jax.random.normal(jax.random.fold_in(key, 8), (TOTAL_ROWS, OUTPUT_FEATURES), jnp.float32), -4.0, 4.0)
    return (body_values * column_scale[None, :]).astype(jnp.bfloat16)


def block_scale(own_key, dims, cuts, smallest, top_value):
    def one(dim, shards_of):
        draws = jax.random.uniform(jax.random.fold_in(jax.random.fold_in(own_key, 6), dim), (shards_of,), jnp.float32, smallest / len(cuts), top_value / len(cuts))
        return jnp.repeat(jnp.exp(draws), dims[dim] // shards_of).reshape((-1,) + (1,) * (len(dims) - dim - 1))

    level = one(*cuts[0])
    for cut in cuts[1:]:
        level = level * one(*cut)
    return level


def noise(own_key, dims, deviation, most, cuts=(), held_as=jnp.bfloat16):
    factor_of = block_scale(own_key, dims, cuts, -0.22, 0.18) if cuts else 1.0
    array = jax.random.normal(own_key, dims, jnp.float32) * deviation * factor_of
    return jnp.minimum(jnp.maximum(array, -most), most).astype(held_as)


def setup_inputs(seed: int = 0) -> dict:
    key_list = jax.random.split(jax.random.key(seed), 14)
    return {
        "state_input": noise(key_list[0], (TOTAL_ROWS, INNER_CHANNELS), 1.0, 6.0, ((0, 128),)),
        "gate_values": noise(key_list[1], (TOTAL_ROWS, INNER_CHANNELS), 1.0, 6.0, ((0, 128),)),
        "input_matrix": draw_input_matrix(jax.random.fold_in(key_list[13], 71), 0),
        "readout_matrix": noise(key_list[3], (TOTAL_ROWS, G * N), 0.3, 1.1953125, ((0, 128),)),
        "step_unbiased": draw_step_unbiased(jax.random.fold_in(key_list[13], 71), 0),
        "step_bias": jnp.clip(jax.random.uniform(key_list[5], (H,), jnp.float32, -1.0, 0.5), -1.0, 0.5),
        "decay_rate_log": draw_decay_rate_log(jax.random.fold_in(key_list[13], 71), 0),
        "skip_coefficients": jnp.clip(jnp.exp(jax.random.uniform(key_list[7], (H,), jnp.float32, math.log(3.0), math.log(10.0))), 3.0, 10.0),
        "norm_gain": draw_norm_gain(jax.random.fold_in(key_list[13], 71), 0),
        "adapter_down": noise(key_list[9], (ADAPTER_RANK, INNER_CHANNELS), INNER_CHANNELS ** -0.5, 0.09375),
        "adapter_up": noise(key_list[10], (ADAPTER_RANK, OUTPUT_FEATURES), ADAPTER_RANK ** -0.5, 0.75),
        "projection_weight": noise(key_list[11], (OUTPUT_FEATURES, INNER_CHANNELS), INNER_CHANNELS ** -0.5, 0.09375, ((0, 128),)),
        "output_cotangent": draw_output_cotangent(jax.random.fold_in(key_list[13], 71), 0),
    }


EPS_NORM = 1e-05
CLIP_EPSILON = 1e-06
ADAPTER_SCALE = 2.0

def heads_of(grouped):
    lead = grouped.shape[:-2]
    spread = jnp.broadcast_to(grouped[..., :, None, :], lead + (G, H // G, grouped.shape[-1]))
    return spread.reshape(lead + (H, grouped.shape[-1]))

def block_pieces(cum_decay, block_b, block_c):
    b_float = block_b.astype(jnp.float32)
    c_float = block_c.astype(jnp.float32)
    inner_prod = jnp.einsum('ign,jgn->gij', c_float, b_float)
    inner_prod = jnp.broadcast_to(inner_prod[:, None], (G, H // G, Q, Q)).reshape(H, Q, Q)
    cum_heads = cum_decay.T
    gap_logs = cum_heads[:, :, None] - cum_heads[:, None, :]
    causal = lax.broadcasted_iota(jnp.int32, (Q, Q), 0) >= lax.broadcasted_iota(jnp.int32, (Q, Q), 1)
    weights = jnp.where(causal[None], jnp.exp(jnp.where(causal[None], gap_logs, 0.0)), 0.0)
    scores = (inner_prod * weights).astype(jnp.bfloat16)
    block_total = cum_decay[-1]
    b_weighted = (jnp.exp(block_total[None, :] - cum_decay)[:, :, None] * heads_of(b_float)).astype(jnp.bfloat16)
    return (scores, b_weighted)

def forward_block(run_state, block_item):
    xdt_block, block_b, block_c, cum_decay = block_item
    scores, b_weighted = block_pieces(cum_decay, block_b, block_c)
    xdt_float = xdt_block.astype(jnp.float32)
    intra_part = jnp.einsum('hij,jhp->ihp', scores.astype(jnp.float32), xdt_float)
    incoming_bf = run_state.astype(jnp.bfloat16).astype(jnp.float32)
    c_heads = heads_of(block_c.astype(jnp.float32))
    inter_part = jnp.exp(cum_decay)[:, :, None] * jnp.einsum('ihn,hnp->ihp', c_heads, incoming_bf)
    block_state = jnp.einsum('jhn,jhp->hnp', b_weighted.astype(jnp.float32), xdt_float)
    next_state = jnp.exp(cum_decay[-1])[:, None, None] * run_state + block_state
    return (next_state, intra_part + inter_part)

def backward_block(grad_state, block_item):
    grad_block, block_b, block_c, cum_decay = block_item
    scores, b_weighted = block_pieces(cum_decay, block_b, block_c)
    grad_float = grad_block.astype(jnp.float32)
    intra_back = jnp.einsum('hij,ihp->jhp', scores.astype(jnp.float32), grad_float)
    outgoing_bf = grad_state.astype(jnp.bfloat16).astype(jnp.float32)
    cross_part = jnp.einsum('jhn,hnp->jhp', b_weighted.astype(jnp.float32), outgoing_bf)
    c_heads = heads_of(block_c.astype(jnp.float32))
    c_weighted = (jnp.exp(cum_decay)[:, :, None] * c_heads).astype(jnp.bfloat16)
    block_grad = jnp.einsum('ihn,ihp->hnp', c_weighted.astype(jnp.float32), grad_float)
    next_grad = jnp.exp(cum_decay[-1])[:, None, None] * grad_state + block_grad
    return (next_grad, intra_back + cross_part)

def reference(state_input, gate_values, input_matrix, readout_matrix, step_unbiased, step_bias, decay_rate_log, skip_coefficients, norm_gain, adapter_down, adapter_up, projection_weight, output_cotangent):
    block_count = SEQUENCE_LENGTH // Q
    group_width = INNER_CHANNELS // G
    weight_groups = norm_gain.reshape(G, group_width)

    def one_sequence(seq_item):
        seq_x, seq_z, seq_b, seq_c, seq_dt, sequence_gradient = seq_item
        step_size = jax.nn.softplus(seq_dt + step_bias[None, :])
        cum_decay = jnp.cumsum((-jnp.exp(decay_rate_log)[None, :] * step_size).reshape(block_count, Q, H), axis=1)
        x_heads = seq_x.astype(jnp.float32).reshape(SEQUENCE_LENGTH, H, P_SIZE)
        xdt_all = (x_heads * step_size[:, :, None]).astype(jnp.bfloat16).reshape(block_count, Q, H, P_SIZE)
        b_blocks = seq_b.reshape(block_count, Q, G, N)
        c_blocks = seq_c.reshape(block_count, Q, G, N)
        zero_state = jnp.zeros((H, N, P_SIZE), jnp.float32)
        last_state, ssd_parts = lax.scan(forward_block, zero_state, (xdt_all, b_blocks, c_blocks, cum_decay))
        ssd_out = ssd_parts.reshape(SEQUENCE_LENGTH, H, P_SIZE) + skip_coefficients[None, :, None] * x_heads
        silu_z = jax.nn.silu(seq_z.astype(jnp.float32))
        gated = (ssd_out.reshape(SEQUENCE_LENGTH, INNER_CHANNELS) * silu_z).reshape(SEQUENCE_LENGTH, G, group_width)
        rstd = lax.rsqrt(lax.optimization_barrier(jnp.mean(gated * gated, axis=-1, keepdims=True)) + EPS_NORM)
        normalized = (gated * rstd * weight_groups).reshape(SEQUENCE_LENGTH, INNER_CHANNELS).astype(jnp.bfloat16)
        down_product = lax.dot_general(normalized, adapter_down, (((1,), (1,)), ((), ())), preferred_element_type=jnp.float32).astype(jnp.bfloat16)
        upper_gradient = lax.dot_general(sequence_gradient, adapter_up, (((1,), (1,)), ((), ())), preferred_element_type=jnp.float32).astype(jnp.bfloat16)
        down_portion = ADAPTER_SCALE * lax.dot_general(upper_gradient, normalized, (((0,), (0,)), ((), ())), preferred_element_type=jnp.float32)
        up_portion = ADAPTER_SCALE * lax.dot_general(down_product, sequence_gradient, (((0,), (0,)), ((), ())), preferred_element_type=jnp.float32)
        normed_gradient = jnp.dot(sequence_gradient, projection_weight, preferred_element_type=jnp.float32) + ADAPTER_SCALE * jnp.dot(upper_gradient, adapter_down, preferred_element_type=jnp.float32)
        weighted_grad = normed_gradient.reshape(SEQUENCE_LENGTH, G, group_width) * weight_groups
        d_gated = rstd * weighted_grad - gated * (rstd * rstd * rstd) * lax.optimization_barrier(jnp.mean(gated * weighted_grad, axis=-1, keepdims=True))
        d_ssd = d_gated.reshape(SEQUENCE_LENGTH, INNER_CHANNELS) * silu_z
        d_ssd_bf = d_ssd.reshape(block_count, Q, H, P_SIZE).astype(jnp.bfloat16)
        first_grad, back_parts = lax.scan(backward_block, zero_state, (d_ssd_bf, b_blocks, c_blocks, cum_decay), reverse=True)
        grad_heads = step_size[:, :, None] * back_parts.reshape(SEQUENCE_LENGTH, H, P_SIZE) + skip_coefficients[None, :, None] * d_ssd.reshape(SEQUENCE_LENGTH, H, P_SIZE)
        return (grad_heads.reshape(SEQUENCE_LENGTH, INNER_CHANNELS).astype(jnp.bfloat16), down_portion, up_portion)
    stacked = (state_input.reshape(N_DP, SEQUENCE_LENGTH, INNER_CHANNELS), gate_values.reshape(N_DP, SEQUENCE_LENGTH, INNER_CHANNELS), input_matrix.reshape(N_DP, SEQUENCE_LENGTH, G * N), readout_matrix.reshape(N_DP, SEQUENCE_LENGTH, G * N), step_unbiased.reshape(N_DP, SEQUENCE_LENGTH, H), output_cotangent.reshape(N_DP, SEQUENCE_LENGTH, OUTPUT_FEATURES))
    gradient_sequence, parts_a, parts_b = lax.map(one_sequence, stacked)
    down_total = lax.optimization_barrier(jnp.sum(parts_a, axis=0))
    up_total = lax.optimization_barrier(jnp.sum(parts_b, axis=0))
    adapter_down_gradient = down_total / jnp.maximum(1.0, jnp.sqrt(jnp.mean(down_total * down_total) + CLIP_EPSILON))
    adapter_up_gradient = up_total / jnp.maximum(1.0, jnp.sqrt(jnp.mean(up_total * up_total) + CLIP_EPSILON))
    return (gradient_sequence.reshape(TOTAL_ROWS, INNER_CHANNELS), adapter_down_gradient, adapter_up_gradient)
```

```python
import jax
import jax.numpy as jnp
from jax import lax
from jax.experimental import pallas as pl
from jax.experimental.pallas import tpu as pltpu
from jax.sharding import PartitionSpec as P

H = 64
P_SIZE = 64
N = 128
G = 4
Q = 256
INNER = 4096
OUTF = 2048
RANK = 64
GW = INNER // G
HG = H // G
PAIRS = HG // 2
EPS_NORM = 1e-05
CLIP_EPSILON = 1e-06
SCALE = 2.0
MESH = pl.DeviceIdType.MESH
F32 = jnp.float32
BF16 = jnp.bfloat16
VMEM_LIMIT = 62 * 1024 * 1024


def dot(a, b):
    return lax.dot_general(a, b, (((1,), (0,)), ((), ())), preferred_element_type=F32)


def dot_t(a, b):
    return lax.dot_general(a, b, (((1,), (1,)), ((), ())), preferred_element_type=F32)


def low_lanes(rows):
    return lax.broadcasted_iota(jnp.int32, (rows, 128), 1) < 64


def decay_tables(dtu_ref, bias_ref, alog_ref, cd_ref, cdt_ref):
    step = jax.nn.softplus(dtu_ref[...] + bias_ref[...])
    run = -jnp.exp(alog_ref[...]) * step
    rows = lax.broadcasted_iota(jnp.int32, (Q, H), 0)
    shift = 1
    while shift < Q:
        run = run + jnp.where(rows >= shift, pltpu.roll(run, shift, 0), 0.0)
        shift *= 2
    both = jnp.concatenate([run, step], axis=1)
    cd_ref[...] = both
    cdt_ref[...] = both.T


def group_tables(g, cd_ref, cdt_ref):
    cols = pltpu.roll(cd_ref[...], lax.rem(128 - HG * g, 128), 1)
    cum_rows = cdt_ref[pl.ds(pl.multiple_of(HG * g, 8), HG), :]
    return cols, cum_rows


def pair_lanes(cols, q, low):
    return jnp.where(low, cols[:, 2 * q : 2 * q + 1], cols[:, 2 * q + 1 : 2 * q + 2])


def forward_kernel(
    dtu_ref, bias_ref, alog_ref, skip_ref, x_ref, b_ref, c_ref, s_ref, tot_ref, y_ref, cd_ref, cdt_ref
):
    g = pl.program_id(0)

    @pl.when(g == 0)
    def _():
        decay_tables(dtu_ref, bias_ref, alog_ref, cd_ref, cdt_ref)

    cols, cum_rows = group_tables(g, cd_ref, cdt_ref)
    dts = cols[:, H : H + HG]
    low = low_lanes(Q)
    low_n = low_lanes(N)
    b_t = b_ref[...].astype(F32).T
    prod = dot_t(c_ref[...], b_ref[...])
    ri = lax.broadcasted_iota(jnp.int32, (128, 128), 0)
    ci = lax.broadcasted_iota(jnp.int32, (128, 128), 1)
    p00 = jnp.where(ri >= ci, prod[:128, :128], 0.0)
    p10 = prod[128:, :128]
    p11 = jnp.where(ri >= ci, prod[128:, 128:], 0.0)

    for q in range(PAIRS):
        xp = x_ref[:, q * 128 : (q + 1) * 128].astype(F32)
        xdt = (xp * pair_lanes(dts, q, low)).astype(BF16)
        tops, lows, states = [], [], []
        for h in (2 * q, 2 * q + 1):
            col = cols[:, h : h + 1]
            row = cum_rows[h : h + 1, :]
            s00 = (p00 * jnp.exp(jnp.minimum(col[:128] - row[:, :128], 0.0))).astype(BF16)
            s10 = (p10 * jnp.exp(jnp.minimum(col[128:] - row[:, :128], 0.0))).astype(BF16)
            s11 = (p11 * jnp.exp(jnp.minimum(col[128:] - row[:, 128:], 0.0))).astype(BF16)
            tops.append(dot(s00, xdt[:128]))
            lows.append(dot(jnp.concatenate([s10, s11], axis=1), xdt))
            bw = (b_t * jnp.exp(row[:, Q - 1 : Q] - row)).astype(BF16)
            states.append(dot(bw, xdt))
        skip = skip_ref[:, q * 128 : (q + 1) * 128]
        sl = slice(q * 128, (q + 1) * 128)
        y_ref[:128, sl] = jnp.where(low[:128], tops[0], tops[1]) + skip * xp[:128]
        y_ref[128:, sl] = jnp.where(low[:128], lows[0], lows[1]) + skip * xp[128:]
        s_ref[0, q] = jnp.where(low_n, states[0], states[1]).astype(BF16)
        tot_ref[0, q] = pair_lanes(cols[Q - 8 :, :HG], q, low_lanes(8))[7:8] + jnp.zeros((8, 128), F32)


def whole(shape):
    zeros = (0,) * len(shape)
    return pl.BlockSpec(shape, lambda g: zeros)


def local_forward(dtu, bias, alog, skip, x, b, c):
    col = lambda w: pl.BlockSpec((Q, w), lambda g: (0, g))
    return pl.pallas_call(
        forward_kernel,
        grid=(G,),
        in_specs=[
            whole((Q, H)),
            whole((1, H)),
            whole((1, H)),
            pl.BlockSpec((1, GW), lambda g: (0, g)),
            col(GW),
            col(N),
            col(N),
        ],
        out_specs=[
            pl.BlockSpec((1, PAIRS, N, 128), lambda g: (g, 0, 0, 0)),
            pl.BlockSpec((1, PAIRS, 8, 128), lambda g: (g, 0, 0, 0)),
            col(GW),
            whole((Q, 128)),
            whole((128, Q)),
        ],
        out_shape=[
            jax.ShapeDtypeStruct((G, PAIRS, N, 128), BF16),
            jax.ShapeDtypeStruct((G, PAIRS, 8, 128), F32),
            jax.ShapeDtypeStruct((Q, INNER), F32),
            jax.ShapeDtypeStruct((Q, 128), F32),
            jax.ShapeDtypeStruct((128, Q), F32),
        ],
        name="local_forward",
    )(dtu, bias, alog, skip, x, b, c)


class Place:
    def __init__(self):
        self.dp = lax.axis_index("dp")
        self.ctx = lax.axis_index("ctx")
        self.y = lax.div(self.dp, 4)
        self.z = lax.rem(self.dp, 4)
        self.x = lax.div(self.ctx, 2)
        self.c = lax.rem(self.ctx, 2)

    def coord(self, axis):
        return {"x": self.x, "y": self.y, "z": self.z}[axis]

    def along(self, axis, step):
        if axis == "x":
            return {"dp": self.dp, "ctx": lax.rem(self.x + step, 4) * 2 + self.c}
        if axis == "y":
            return {"dp": lax.rem(self.y + step, 4) * 4 + self.z, "ctx": self.ctx}
        return {"dp": self.y * 4 + lax.rem(self.z + step, 4), "ctx": self.ctx}

    def partner(self):
        return {"dp": self.dp, "ctx": self.x * 2 + 1 - self.c}

    def position(self, step):
        return lax.rem(self.ctx + step, 8)


def greet(devices):
    barrier = pltpu.get_barrier_semaphore()
    for device in devices:
        pl.semaphore_signal(barrier, inc=1, device_id=device, device_id_type=MESH)
    pl.semaphore_wait(barrier, len(devices))


def send(src, dst, sems, slot, device):
    copy = pltpu.make_async_remote_copy(
        src_ref=src,
        dst_ref=dst,
        send_sem=sems[0].at[slot],
        recv_sem=sems[1].at[slot],
        device_id=device,
        device_id_type=MESH,
    )
    copy.start()
    return copy


class Exchange:
    def __init__(self, place, s_ref, tot_ref, out_ref, got, got_tot, made, sems):
        self.place, self.s, self.tot, self.out = place, s_ref, tot_ref, out_ref
        self.got, self.got_tot, self.made, self.sems = got, got_tot, made, sems

    def scatter(self):
        me = self.place.ctx
        self.first = []
        for o in range(1, 8):
            k = self.place.position(o)
            device = {"dp": self.place.dp, "ctx": k}
            self.first.append(send(self.tot.at[:, k], self.got_tot.at[me], self.sems, 7 + o - 1, device))
            self.first.append(send(self.s.at[:, k], self.got.at[me], self.sems, o - 1, device))
        self.got[me] = self.s[:, me]
        self.got_tot[me] = self.tot[:, me]

    def combine(self, reverse):
        for copy in self.first:
            copy.wait()
        order = range(7, -1, -1) if reverse else range(8)
        for g in range(G):
            run = jnp.zeros((N, 128), F32)
            for j in order:
                self.made[j, g] = run.astype(BF16)
                run = jnp.exp(self.got_tot[j, g, 0:1]) * run + self.got[j, g].astype(F32)
        me = self.place.ctx
        self.second = []
        for o in range(1, 8):
            j = self.place.position(o)
            self.second.append(
                send(
                    self.made.at[j],
                    self.out.at[:, me],
                    self.sems,
                    14 + o - 1,
                    {"dp": self.place.dp, "ctx": j},
                )
            )
        self.out[:, me] = self.made[me]

    def finish(self):
        for copy in self.second:
            copy.wait()


EXCHANGE_SCRATCH = [
    pltpu.VMEM((8, G, N, 128), BF16),
    pltpu.VMEM((8, G, 8, 128), F32),
    pltpu.VMEM((8, G, N, 128), BF16),
    pltpu.SemaphoreType.DMA((21,)),
    pltpu.SemaphoreType.DMA((21,)),
]

PARTS = (
    (("x", "y", "z"), 0, 1664),
    (("y", "z", "x"), 1664, 768),
    (("x", "z", "y"), 2432, 1664),
)


class Part:
    def __init__(self, place, own_ref, out_ref, order, start, width, sems, base):
        self.place, self.own, self.out = place, own_ref, out_ref
        self.order, self.start, self.width = order, start, width
        self.first = (width // 128 + 1) // 2 * 128
        self.sems, self.slot = sems, base
        self.sent = []

    def view(self, stage, step, half=None):
        picks = {}
        for i, axis in enumerate(self.order):
            if i < stage:
                picks[axis] = slice(None)
            elif i == stage:
                picks[axis] = lax.rem(self.place.coord(axis) + step, 4)
            else:
                picks[axis] = self.place.coord(axis)
        c0, w = self.start, self.width
        if half == 0:
            w = self.first
        elif half == 1:
            c0, w = c0 + self.first, w - self.first
        return (picks["y"], picks["z"], picks["x"], self.place.c, slice(None), pl.ds(c0, w))

    def push(self, view, device, src=None):
        ref = self.out.at[view]
        copy = send(ref if src is None else src, ref, self.sems, self.slot, device)
        self.slot += 1
        self.sent.append(copy)
        return copy

    def hop_one(self, stage):
        axis = self.order[stage]
        view = self.view(stage, 0)
        src = None
        if stage == 0:
            src = self.own.at[:, pl.ds(self.start, self.width)]
        self.from_left = self.push(view, self.place.along(axis, 1), src)
        self.from_right = self.push(view, self.place.along(axis, 3), src)

    def hop_two(self, stage):
        axis = self.order[stage]
        self.from_left.wait_recv()
        far = [self.push(self.view(stage, 3, 0), self.place.along(axis, 1))]
        self.from_right.wait_recv()
        far.append(self.push(self.view(stage, 1, 1), self.place.along(axis, 3)))
        self.far = far

    def arrive(self):
        for copy in self.far:
            copy.wait_recv()

    def share(self, stage, step, half=None):
        return self.push(self.view(stage, step, half), self.place.partner())


SLOTS_PER_PART = 17


def gather_kernel(
    w_ref, s_ref, tot_ref, full_ref, inc_ref, got, got_tot, made, x_send, x_recv, send_sem, recv_sem, own_sem
):
    place = Place()
    near = [place.along(axis, step) for axis in "yz" for step in (1, 3)]
    greet(near + [{"dp": place.dp, "ctx": place.position(o)} for o in range(1, 8)])
    sems = (send_sem, recv_sem)
    parts = [
        Part(place, w_ref, full_ref, order, start, width, sems, i * SLOTS_PER_PART)
        for i, (order, start, width) in enumerate(PARTS)
    ]
    states = Exchange(place, s_ref, tot_ref, inc_ref, got, got_tot, made, (x_send, x_recv))
    own = pltpu.make_async_copy(w_ref, full_ref.at[place.y, place.z, place.x, place.c], own_sem)
    own.start()
    for part in parts:
        part.hop_one(0)
    states.scatter()
    for part in parts:
        part.hop_two(0)
    own.wait()
    for part in parts:
        part.arrive()
        part.hop_one(1)
    for part in parts:
        part.hop_two(1)
    for part in parts:
        part.arrive()
        part.hop_one(2)
    shared = [part.share(2, 0) for part in parts]
    states.combine(False)
    for part in parts:
        part.hop_two(2)
        shared.append(part.share(2, 3))
        shared.append(part.share(2, 1))
    for part in parts:
        part.arrive()
        shared.append(part.share(2, 2))
    for copy in shared:
        copy.wait_recv()
    for part in parts:
        for copy in part.sent:
            copy.wait_send()
    states.finish()


def gather_weight_and_states(w, s, tot):
    vmem = pl.BlockSpec(memory_space=pltpu.VMEM)
    return pl.pallas_call(
        gather_kernel,
        in_specs=[vmem, vmem, vmem],
        out_specs=[pl.BlockSpec(memory_space=pl.ANY), vmem],
        out_shape=[
            jax.ShapeDtypeStruct((4, 4, 4, 2, 16, INNER), BF16),
            jax.ShapeDtypeStruct((G, PAIRS, N, 128), BF16),
        ],
        scratch_shapes=EXCHANGE_SCRATCH
        + [
            pltpu.SemaphoreType.DMA((3 * SLOTS_PER_PART,)),
            pltpu.SemaphoreType.DMA((3 * SLOTS_PER_PART,)),
            pltpu.SemaphoreType.DMA,
        ],
        compiler_params=pltpu.CompilerParams(collective_id=1, has_side_effects=True),
        name="gather_weight_and_states",
    )(w, s, tot)


def reduce_kernel(
    g_ref,
    tot_ref,
    sa_ref,
    sb_ref,
    out_ref,
    da_ref,
    db_ref,
    got,
    got_tot,
    made,
    x_send,
    x_recv,
    a0,
    b0,
    a1,
    b1,
    ra1,
    rb1,
    a2,
    b2,
    ra2,
    rb2,
    ra3,
    rb3,
    sq,
    rsq,
    send_sem,
    recv_sem,
):
    place = Place()
    lines = [place.along(axis, step) for axis in "yz" for step in (1, 2, 3)]
    greet(lines + [{"dp": place.dp, "ctx": place.position(o)} for o in range(1, 8)])
    states = Exchange(place, g_ref, tot_ref, out_ref, got, got_tot, made, (x_send, x_recv))
    sems = (send_sem, recv_sem)
    slots = iter(range(64))
    push = lambda src, dst, device: send(src, dst, sems, next(slots), device)
    half = RANK // 2
    mine = pl.ds(pl.multiple_of(place.c * half, half), half)
    theirs = pl.ds(pl.multiple_of((1 - place.c) * half, half), half)
    partner = place.partner()

    first = [push(sa_ref.at[theirs], a0, partner), push(sb_ref.at[theirs], b0, partner)]
    states.scatter()
    for copy in first:
        copy.wait()
    a0[...] += sa_ref[mine]
    b0[...] += sb_ref[mine]

    def spread(axis, wide, narrow, a, b, ra, rb):
        copies = []
        for o in (1, 2, 3):
            to = lax.rem(place.coord(axis) + o, 4)
            device = place.along(axis, o)
            ca = pl.ds(pl.multiple_of(to * wide, 128), wide)
            cb = pl.ds(pl.multiple_of(to * narrow, 128), narrow)
            copies.append(push(a.at[:, ca], ra.at[o - 1], device))
            copies.append(push(b.at[:, cb], rb.at[o - 1], device))
        return copies

    def summed(axis, wide, narrow, a, b, ra, rb):
        own = place.coord(axis)
        ca = pl.ds(pl.multiple_of(own * wide, 128), wide)
        cb = pl.ds(pl.multiple_of(own * narrow, 128), narrow)
        return (
            a[:, ca] + (ra[0] + ra[1] + ra[2]),
            b[:, cb] + (rb[0] + rb[1] + rb[2]),
        )

    copies = spread("y", 1024, 512, a0, b0, ra1, rb1)
    states.combine(True)
    for copy in copies:
        copy.wait()
    a1[...], b1[...] = summed("y", 1024, 512, a0, b0, ra1, rb1)
    copies = spread("z", 256, 128, a1, b1, ra2, rb2)
    for copy in copies:
        copy.wait()
    a2[mine], b2[mine] = summed("z", 256, 128, a1, b1, ra2, rb2)
    copies = []
    for o in (1, 2, 3):
        device = place.along("x", o)
        copies.append(push(a2.at[mine], ra3.at[o - 1], device))
        copies.append(push(b2.at[mine], rb3.at[o - 1], device))
    for copy in copies:
        copy.wait()
    a2[mine] += ra3[0] + ra3[1] + ra3[2]
    b2[mine] += rb3[0] + rb3[1] + rb3[2]
    copies = [push(a2.at[mine], a2.at[mine], partner), push(b2.at[mine], b2.at[mine], partner)]
    for copy in copies:
        copy.wait()
    a = a2[...]
    b = b2[...]
    row = lax.broadcasted_iota(jnp.int32, (8, 128), 0)
    sq[0] = jnp.where(row == 0, jnp.sum(a * a), jnp.sum(b * b))
    for i, axis in enumerate("yz"):
        copies = [push(sq.at[i], rsq.at[i, o - 1], place.along(axis, o)) for o in (1, 2, 3)]
        for copy in copies:
            copy.wait()
        sq[i + 1] = sq[i] + (rsq[i, 0] + rsq[i, 1] + rsq[i, 2])
    total = sq[2]
    root_a = jnp.sqrt(total[0:1, 0:1] / (RANK * INNER) + CLIP_EPSILON)
    root_b = jnp.sqrt(total[1:2, 0:1] / (RANK * OUTF) + CLIP_EPSILON)
    da_ref[...] = a / jnp.maximum(1.0, root_a)
    db_ref[...] = b / jnp.maximum(1.0, root_b)
    states.finish()


def reduce_sums_and_states(grad, tot, sa, sb):
    vmem = pl.BlockSpec(memory_space=pltpu.VMEM)
    half = RANK // 2
    return pl.pallas_call(
        reduce_kernel,
        in_specs=[vmem] * 4,
        out_specs=[vmem] * 3,
        out_shape=[
            jax.ShapeDtypeStruct((G, PAIRS, N, 128), BF16),
            jax.ShapeDtypeStruct((RANK, 256), F32),
            jax.ShapeDtypeStruct((RANK, 128), F32),
        ],
        scratch_shapes=EXCHANGE_SCRATCH
        + [
            pltpu.VMEM((half, INNER), F32),
            pltpu.VMEM((half, OUTF), F32),
            pltpu.VMEM((half, 1024), F32),
            pltpu.VMEM((half, 512), F32),
            pltpu.VMEM((3, half, 1024), F32),
            pltpu.VMEM((3, half, 512), F32),
            pltpu.VMEM((RANK, 256), F32),
            pltpu.VMEM((RANK, 128), F32),
            pltpu.VMEM((3, half, 256), F32),
            pltpu.VMEM((3, half, 128), F32),
            pltpu.VMEM((3, half, 256), F32),
            pltpu.VMEM((3, half, 128), F32),
            pltpu.VMEM((3, 8, 128), F32),
            pltpu.VMEM((2, 3, 8, 128), F32),
            pltpu.SemaphoreType.DMA((32,)),
            pltpu.SemaphoreType.DMA((32,)),
        ],
        compiler_params=pltpu.CompilerParams(collective_id=2, has_side_effects=True),
        name="reduce_sums_and_states",
    )(grad, tot, sa, sb)


def middle_kernel(
    y_ref,
    z_ref,
    c_ref,
    inc_ref,
    cd_ref,
    cdt_ref,
    gain_ref,
    w_ref,
    cot_ref,
    down_ref,
    up_ref,
    d_ref,
    grad_ref,
    sa_ref,
    sb_ref,
    ssd,
    dn,
    normed,
    up_t,
    up_row,
    down_t,
):
    g = pl.program_id(0)

    @pl.when(g == 0)
    def _():
        up_t[...] = dot_t(up_ref[...], cot_ref[...]).astype(BF16)
        up_row[...] = dot_t(cot_ref[...], up_ref[...]).astype(BF16)
        down_t[...] = jnp.zeros_like(down_t)

    cols, cum_rows = group_tables(g, cd_ref, cdt_ref)
    grow = jnp.exp(cols[:, :HG])
    low = low_lanes(Q)
    low_n = low_lanes(N)
    cg = c_ref[...]
    for q in range(PAIRS):
        sl = slice(q * 128, (q + 1) * 128)
        ssd[:, sl] = y_ref[:, sl] + pair_lanes(grow, q, low) * dot(cg, inc_ref[0, q])
    for i in range(GW // 256):
        sl = slice(i * 256, (i + 1) * 256)
        dn[:, sl] = dot(cot_ref[...], w_ref[:, sl]) + SCALE * dot(up_row[...], down_ref[:, sl])

    gain = gain_ref[...]
    rows = 16

    def chunk(i, carry):
        at = pl.ds(pl.multiple_of(i * rows, rows), rows)
        zf = z_ref[at, :].astype(F32)
        silu = zf / (1.0 + jnp.exp(-zf))
        gated = ssd[at, :] * silu
        rstd = lax.rsqrt(jnp.mean(gated * gated, axis=-1, keepdims=True) + EPS_NORM)
        hat = gated * rstd
        normed[at, :] = (hat * gain).astype(BF16)
        wg = dn[at, :] * gain
        slope = jnp.mean(hat * wg, axis=-1, keepdims=True)
        d_ref[at, :] = (rstd * (wg - hat * slope) * silu).astype(BF16)
        return carry

    lax.fori_loop(0, Q // rows, chunk, 0)

    c_t = cg.astype(F32).T
    for q in range(PAIRS):
        dp = d_ref[:, q * 128 : (q + 1) * 128]
        halves = []
        for h in (2 * q, 2 * q + 1):
            cw = (c_t * jnp.exp(cum_rows[h : h + 1, :])).astype(BF16)
            halves.append(dot(cw, dp))
        grad_ref[0, q] = jnp.where(low_n, halves[0], halves[1]).astype(BF16)
    sa_ref[...] = SCALE * dot(up_t[...], normed[...])
    down_t[...] += dot_t(down_ref[...], normed[...])

    @pl.when(g == G - 1)
    def _():
        sb_ref[...] = SCALE * dot(down_t[...].astype(BF16), cot_ref[...])


def middle(y, z, c, inc, cd, cdt, gain, w, cot, down, up):
    col = lambda w_: pl.BlockSpec((Q, w_), lambda g: (0, g))
    return pl.pallas_call(
        middle_kernel,
        grid=(G,),
        in_specs=[
            col(GW),
            col(GW),
            col(N),
            pl.BlockSpec((1, PAIRS, N, 128), lambda g: (g, 0, 0, 0)),
            whole((Q, 128)),
            whole((128, Q)),
            pl.BlockSpec((1, GW), lambda g: (0, g)),
            pl.BlockSpec((OUTF, GW), lambda g: (0, g)),
            whole((Q, OUTF)),
            pl.BlockSpec((RANK, GW), lambda g: (0, g)),
            whole((RANK, OUTF)),
        ],
        out_specs=[
            col(GW),
            pl.BlockSpec((1, PAIRS, N, 128), lambda g: (g, 0, 0, 0)),
            pl.BlockSpec((RANK, GW), lambda g: (0, g)),
            whole((RANK, OUTF)),
        ],
        out_shape=[
            jax.ShapeDtypeStruct((Q, INNER), BF16),
            jax.ShapeDtypeStruct((G, PAIRS, N, 128), BF16),
            jax.ShapeDtypeStruct((RANK, INNER), F32),
            jax.ShapeDtypeStruct((RANK, OUTF), F32),
        ],
        scratch_shapes=[
            pltpu.VMEM((Q, GW), F32),
            pltpu.VMEM((Q, GW), F32),
            pltpu.VMEM((Q, GW), BF16),
            pltpu.VMEM((RANK, Q), BF16),
            pltpu.VMEM((Q, RANK), BF16),
            pltpu.VMEM((RANK, Q), F32),
        ],
        compiler_params=pltpu.CompilerParams(vmem_limit_bytes=48 * 1024 * 1024),
        name="middle",
    )(y, z, c, inc, cd, cdt, gain, w, cot, down, up)


def backward_kernel(d_ref, b_ref, c_ref, outg_ref, cd_ref, cdt_ref, skip_ref, o_ref):
    g = pl.program_id(0)
    cols, cum_rows = group_tables(g, cd_ref, cdt_ref)
    dts = cols[:, H : H + HG]
    fade = jnp.exp(cols[Q - 1 : Q, :HG] - cols[:, :HG])
    low = low_lanes(Q)
    bg = b_ref[...]
    prod = dot_t(bg, c_ref[...])
    ri = lax.broadcasted_iota(jnp.int32, (128, 128), 0)
    ci = lax.broadcasted_iota(jnp.int32, (128, 128), 1)
    p00 = jnp.where(ci >= ri, prod[:128, :128], 0.0)
    p01 = prod[:128, 128:]
    p11 = jnp.where(ci >= ri, prod[128:, 128:], 0.0)
    for q in range(PAIRS):
        sl = slice(q * 128, (q + 1) * 128)
        dp = d_ref[:, sl]
        tops, lows = [], []
        for h in (2 * q, 2 * q + 1):
            col = cols[:, h : h + 1]
            row = cum_rows[h : h + 1, :]
            s00 = (p00 * jnp.exp(jnp.minimum(row[:, :128] - col[:128], 0.0))).astype(BF16)
            s01 = (p01 * jnp.exp(jnp.minimum(row[:, 128:] - col[:128], 0.0))).astype(BF16)
            s11 = (p11 * jnp.exp(jnp.minimum(row[:, 128:] - col[128:], 0.0))).astype(BF16)
            tops.append(dot(jnp.concatenate([s00, s01], axis=1), dp))
            lows.append(dot(s11, dp[128:]))
        cross = pair_lanes(fade, q, low) * dot(bg, outg_ref[0, q])
        dt = pair_lanes(dts, q, low)
        skip = skip_ref[:, sl]
        top = jnp.where(low[:128], tops[0], tops[1]) + cross[:128]
        bottom = jnp.where(low[:128], lows[0], lows[1]) + cross[128:]
        o_ref[:128, sl] = (dt[:128] * top + skip * dp[:128].astype(F32)).astype(BF16)
        o_ref[128:, sl] = (dt[128:] * bottom + skip * dp[128:].astype(F32)).astype(BF16)


def local_backward(d, b, c, outg, cd, cdt, skip):
    col = lambda w: pl.BlockSpec((Q, w), lambda g: (0, g))
    return pl.pallas_call(
        backward_kernel,
        grid=(G,),
        in_specs=[
            col(GW),
            col(N),
            col(N),
            pl.BlockSpec((1, PAIRS, N, 128), lambda g: (g, 0, 0, 0)),
            whole((Q, 128)),
            whole((128, Q)),
            pl.BlockSpec((1, GW), lambda g: (0, g)),
        ],
        out_specs=col(GW),
        out_shape=jax.ShapeDtypeStruct((Q, INNER), BF16),
        name="local_backward",
    )(d, b, c, outg, cd, cdt, skip)


def on_device(x, z, b, c, dtu, bias, alog, skip, gain, down, up, w, cot):
    skip_cols = jnp.broadcast_to(skip[:, None], (H, P_SIZE)).reshape(1, INNER)
    s, tot, y, cd, cdt = local_forward(
        dtu, bias.reshape(1, H), alog.reshape(1, H), skip_cols, x, b, c
    )
    full, inc = gather_weight_and_states(w, s, tot)
    d, grad, sa, sb = middle(
        y, z, c, inc, cd, cdt, gain.reshape(1, INNER), full.reshape(OUTF, INNER), cot, down, up
    )
    outg, da, db = reduce_sums_and_states(grad, tot, sa, sb)
    dx = local_backward(d, b, c, outg, cd, cdt, skip_cols)
    place = lax.axis_index("ctx")
    da = lax.dynamic_slice_in_dim(da, place * 32, 32, 1)
    db = lax.dynamic_slice_in_dim(db, place * 16, 16, 1)
    return dx, da, db


def solution(mesh):
    rows = P(("dp", "ctx"), None)
    placed = (rows,) * 5 + (P(),) * 6 + (rows, rows)
    return jax.shard_map(
        on_device,
        mesh=mesh,
        in_specs=placed,
        out_specs=(rows, P(None, ("dp", "ctx")), P(None, ("dp", "ctx"))),
        check_vma=False,
    )
```

```python
import jax
import jax.numpy as jnp
from jax import lax
from jax.experimental import pallas as pl
from jax.experimental.pallas import tpu as pltpu
from jax.sharding import PartitionSpec as P

H = 64
P_SIZE = 64
N = 128
G = 4
Q = 256
INNER = 4096
OUTF = 2048
RANK = 64
GW = INNER // G
HG = H // G
PAIRS = HG // 2
EPS_NORM = 1e-05
CLIP_EPSILON = 1e-06
SCALE = 2.0
MESH = pl.DeviceIdType.MESH
F32 = jnp.float32
BF16 = jnp.bfloat16
VMEM_LIMIT = 62 * 1024 * 1024


def dot(a, b):
    return lax.dot_general(a, b, (((1,), (0,)), ((), ())), preferred_element_type=F32)


def dot_t(a, b):
    return lax.dot_general(a, b, (((1,), (1,)), ((), ())), preferred_element_type=F32)


def low_lanes(rows):
    return lax.broadcasted_iota(jnp.int32, (rows, 128), 1) < 64


def pair_cols(cd_ref, p):
    return pltpu.roll(cd_ref[...], lax.rem(128 - 2 * p, 128), 1)


def pair_lanes(cols, at, low):
    return jnp.where(low, cols[:, at : at + 1], cols[:, at + 1 : at + 2])


def lanes_at(p):
    return pl.ds(pl.multiple_of(p * 128, 128), 128)


class Place:
    def __init__(self):
        self.dp = lax.axis_index("dp")
        self.ctx = lax.axis_index("ctx")
        self.y = lax.div(self.dp, 4)
        self.z = lax.rem(self.dp, 4)
        self.x = lax.div(self.ctx, 2)
        self.c = lax.rem(self.ctx, 2)

    def coord(self, axis):
        return {"x": self.x, "y": self.y, "z": self.z}[axis]

    def along(self, axis, step):
        if axis == "x":
            return {"dp": self.dp, "ctx": lax.rem(self.x + step, 4) * 2 + self.c}
        if axis == "y":
            return {"dp": lax.rem(self.y + step, 4) * 4 + self.z, "ctx": self.ctx}
        return {"dp": self.y * 4 + lax.rem(self.z + step, 4), "ctx": self.ctx}

    def partner(self):
        return {"dp": self.dp, "ctx": self.x * 2 + 1 - self.c}

    def position(self, step):
        return lax.rem(self.ctx + step, 8)


def greet(devices):
    barrier = pltpu.get_barrier_semaphore()
    for device in devices:
        pl.semaphore_signal(barrier, inc=1, device_id=device, device_id_type=MESH)
    return lambda: pl.semaphore_wait(barrier, len(devices))


class Link:
    def __init__(self, send_sem, recv_sem):
        self.send_sem, self.recv_sem, self.used, self.sent = send_sem, recv_sem, 0, []

    def push(self, src, dst, device):
        copy = pltpu.make_async_remote_copy(
            src_ref=src,
            dst_ref=dst,
            send_sem=self.send_sem.at[self.used],
            recv_sem=self.recv_sem.at[self.used],
            device_id=device,
            device_id_type=MESH,
        )
        self.used += 1
        copy.start()
        self.sent.append(copy)
        return copy

    def settle(self, copies):
        for copy in copies:
            copy.wait_send()
        self.sent = [old for old in self.sent if all(old is not copy for copy in copies)]

    def drain(self):
        for copy in self.sent:
            copy.wait_send()


class Exchange:
    def __init__(self, place, link, own, tots, got, made, out, reverse):
        self.place, self.link, self.own, self.tots = place, link, own, tots
        self.got, self.made, self.out, self.reverse = got, made, out, reverse
        self.first, self.second = {}, {}

    def peer(self, k):
        return {"dp": self.place.dp, "ctx": k}

    def scatter(self, g):
        me = self.place.ctx
        self.first[g] = []
        for o in range(1, 8):
            k = self.place.position(o)
            self.first[g].append(self.link.push(self.own.at[g, k], self.got.at[me, g], self.peer(k)))
        self.got[me, g] = self.own[g, me]

    def combine(self, g):
        for copy in self.first[g]:
            copy.wait_recv()
        run = jnp.zeros((N, 128), F32)
        for j in range(7, -1, -1) if self.reverse else range(8):
            self.made[j, g] = run.astype(BF16)
            run = jnp.exp(self.tots[j, g, 0:1]) * run + self.got[j, g].astype(F32)
        me = self.place.ctx
        self.second[g] = []
        for o in range(1, 8):
            j = self.place.position(o)
            self.second[g].append(self.link.push(self.made.at[j, g], self.out.at[g, me], self.peer(j)))
        self.out[g, me] = self.made[me, g]

    def finish(self, g):
        for copy in self.second[g]:
            copy.wait_recv()


PARTS = (
    (("x", "y", "z"), 0, 3),
    (("y", "z", "x"), 3, 2),
    (("x", "z", "y"), 5, 3),
)


class Part:
    def __init__(self, place, link, buf, order, start, tiles):
        self.place, self.link, self.buf = place, link, buf
        self.order, self.start, self.tiles = order, start, tiles
        self.near, self.far = {}, {}

    def view(self, stage, step, group=None, groups=None, tiles=None):
        picks = {}
        for i, axis in enumerate(self.order):
            if i < stage:
                picks[axis] = slice(None)
            elif i == stage:
                picks[axis] = lax.rem(self.place.coord(axis) + step, 4)
            else:
                picks[axis] = self.place.coord(axis)
        lo, count = (0, self.tiles) if tiles is None else tiles
        where = groups if group is None else group
        if where is None:
            where = slice(None)
        return self.buf.at[
            picks["y"],
            picks["z"],
            picks["x"],
            self.place.c,
            where,
            slice(None),
            pl.ds((self.start + lo) * 128, count * 128),
        ]

    def push(self, view, device):
        return self.link.push(view, view, device)

    def hop_one(self, stage, g=None):
        axis = self.order[stage]
        view = self.view(stage, 0, g)
        self.near[stage, g] = (
            self.push(view, self.place.along(axis, 1)),
            self.push(view, self.place.along(axis, 3)),
        )

    def cut(self, g):
        if g is None:
            return {"groups": slice(0, 2)}, {"groups": slice(2, 4)}
        lo = (self.tiles + 1 - g % 2) // 2
        low = {"group": g, "tiles": (0, lo)} if lo else None
        high = {"group": g, "tiles": (lo, self.tiles - lo)} if lo < self.tiles else None
        return low, high

    def hop_two(self, stage, g=None):
        axis = self.order[stage]
        low, high = self.cut(g)
        left, right = self.near[stage, g]
        self.far[stage, g] = []
        left.wait_recv()
        if low is not None:
            self.far[stage, g].append(self.push(self.view(stage, 3, **low), self.place.along(axis, 1)))
        right.wait_recv()
        if high is not None:
            self.far[stage, g].append(self.push(self.view(stage, 1, **high), self.place.along(axis, 3)))

    def arrive(self, stage, g=None):
        for copy in self.far[stage, g]:
            copy.wait_recv()

    def share(self, step, g):
        return self.push(self.view(2, step, g), self.place.partner())


class Weight:
    def __init__(self, place, link, buf):
        self.parts = [Part(place, link, buf, *part) for part in PARTS]
        self.shared = {g: [] for g in range(G)}
        self.plan = (
            (lambda: self.one(0, None),),
            (lambda: self.two(0, None),),
            (lambda: self.one(1, 0, (0, None)), lambda: self.one(1, 1)),
            (lambda: self.two(1, 0), lambda: self.one(1, 2)),
            (lambda: self.last(0), lambda: self.two(1, 1), lambda: self.one(1, 3)),
            (lambda: self.last(1), lambda: self.two(1, 2)),
            (lambda: self.relay(0), lambda: self.last(2), lambda: self.two(1, 3)),
            (lambda: self.relay(1), lambda: self.last(3)),
            (lambda: self.land(0), lambda: self.relay(2)),
            (lambda: self.land(1), lambda: self.relay(3)),
            (lambda: self.land(2),),
            (lambda: self.land(3),),
        )
        self.at = 0

    def step(self):
        for act in self.plan[self.at]:
            act()
        self.at += 1

    def one(self, stage, g, after=None):
        for part in self.parts:
            if after is not None:
                part.arrive(*after)
            part.hop_one(stage, g)

    def two(self, stage, g):
        for part in self.parts:
            part.hop_two(stage, g)

    def last(self, g):
        self.one(2, g, (1, g))
        for part in self.parts:
            self.shared[g].append(part.share(0, g))

    def relay(self, g):
        for part in self.parts:
            part.hop_two(2, g)
        for part in self.parts:
            self.shared[g].append(part.share(3, g))
            self.shared[g].append(part.share(1, g))

    def land(self, g):
        for part in self.parts:
            part.arrive(2, g)
            self.shared[g].append(part.share(2, g))

    def ready(self, g):
        for copy in self.shared[g]:
            copy.wait_recv()


class Sums:
    def __init__(self, place, link, sa, sb, da, db, bufs):
        self.place, self.link, self.sa, self.sb, self.da, self.db = place, link, sa, sb, da, db
        self.bufs = bufs

    def spread(self, axis, wide, narrow, a, b, ra, rb):
        copies = []
        for o in (1, 2, 3):
            to = lax.rem(self.place.coord(axis) + o, 4)
            device = self.place.along(axis, o)
            ca = pl.ds(pl.multiple_of(to * wide, 128), wide)
            cb = pl.ds(pl.multiple_of(to * narrow, 128), narrow)
            copies.append(self.link.push(a.at[:, ca], ra.at[o - 1], device))
            copies.append(self.link.push(b.at[:, cb], rb.at[o - 1], device))
        return copies

    def summed(self, axis, wide, narrow, a, b, ra, rb):
        own = self.place.coord(axis)
        ca = pl.ds(pl.multiple_of(own * wide, 128), wide)
        cb = pl.ds(pl.multiple_of(own * narrow, 128), narrow)
        return (
            a[:, ca] + (ra[0].astype(F32) + ra[1].astype(F32) + ra[2].astype(F32)),
            b[:, cb] + (rb[0].astype(F32) + rb[1].astype(F32) + rb[2].astype(F32)),
        )

    def steps(self):
        place, push = self.place, self.link.push
        a0, b0, a0n, b0n, a1, b1, ra1, rb1, a2, b2, ra2, rb2, ra3, rb3, sq, rsq = self.bufs
        half = RANK // 2
        mine = pl.ds(pl.multiple_of(place.c * half, half), half)
        theirs = pl.ds(pl.multiple_of((1 - place.c) * half, half), half)
        partner = place.partner()

        def arrived(copies):
            for copy in copies:
                copy.wait_recv()

        copies = [push(self.sa.at[theirs], a0, partner), push(self.sb.at[theirs], b0, partner)]
        yield
        arrived(copies)
        a0[...] += self.sa[mine]
        b0[...] += self.sb[mine]
        a0n[...] = a0[...].astype(BF16)
        b0n[...] = b0[...].astype(BF16)
        copies = self.spread("y", 1024, 512, a0n, b0n, ra1, rb1)
        yield
        arrived(copies)
        a1[...], b1[...] = self.summed("y", 1024, 512, a0, b0, ra1, rb1)
        copies = self.spread("z", 256, 128, a1, b1, ra2, rb2)
        yield
        arrived(copies)
        a2[mine], b2[mine] = self.summed("z", 256, 128, a1, b1, ra2, rb2)
        copies = []
        for o in (1, 2, 3):
            device = place.along("x", o)
            copies.append(push(a2.at[mine], ra3.at[o - 1], device))
            copies.append(push(b2.at[mine], rb3.at[o - 1], device))
        yield
        arrived(copies)
        self.link.settle(copies)
        a2[mine] += ra3[0] + ra3[1] + ra3[2]
        b2[mine] += rb3[0] + rb3[1] + rb3[2]
        copies = [push(a2.at[mine], a2.at[mine], partner), push(b2.at[mine], b2.at[mine], partner)]
        yield
        arrived(copies)
        a = a2[...]
        b = b2[...]
        row = lax.broadcasted_iota(jnp.int32, (8, 128), 0)
        sq[0] = jnp.where(row == 0, jnp.sum(a * a), jnp.sum(b * b))
        for i, axis in enumerate("yz"):
            copies = [push(sq.at[i], rsq.at[i, o - 1], place.along(axis, o)) for o in (1, 2, 3)]
            yield
            arrived(copies)
            sq[i + 1] = sq[i] + (rsq[i, 0] + rsq[i, 1] + rsq[i, 2])
        total = sq[2]
        root_a = jnp.sqrt(total[0:1, 0:1] / (RANK * INNER) + CLIP_EPSILON)
        root_b = jnp.sqrt(total[1:2, 0:1] / (RANK * OUTF) + CLIP_EPSILON)
        a = jnp.where(place.ctx >= 4, a2[:, 128:], a2[:, :128]) / jnp.maximum(1.0, root_a)
        b = b2[...] / jnp.maximum(1.0, root_b)
        a = pltpu.roll(a, lax.rem(256 - 32 * place.ctx, 128), 1)
        b = pltpu.roll(b, lax.rem(128 - 16 * place.ctx, 128), 1)
        self.da[...] = a.T[:32, :]
        self.db[...] = b.T[:16, :]
        yield


def decay_tables(dtu_ref, bias_ref, alog_ref, skip_in, cd_ref, rows_ref, tot_ref, skip_ref):
    step = jax.nn.softplus(dtu_ref[...].T + bias_ref[...])
    run = -jnp.exp(alog_ref[...]) * step
    rows = lax.broadcasted_iota(jnp.int32, (Q, H), 0)
    shift = 1
    while shift < Q:
        run = run + jnp.where(rows >= shift, pltpu.roll(run, shift, 0), 0.0)
        shift *= 2
    both = jnp.concatenate([run, step], axis=1)
    cd_ref[...] = both
    turned = both.T
    for h in range(H):
        rows_ref[h] = turned[h : h + 1, :]
    low = low_lanes(8)
    last = both[Q - 1 : Q, :]
    for p in range(H // 2):
        pair = jnp.where(low, last[:, 2 * p : 2 * p + 1], last[:, 2 * p + 1 : 2 * p + 2])
        tot_ref[p // PAIRS, p % PAIRS] = pair
        skip = skip_in[...]
        skip_ref[:, p * 128 : (p + 1) * 128] = jnp.where(
            low[:1], skip[:, 2 * p : 2 * p + 1], skip[:, 2 * p + 1 : 2 * p + 2]
        )


def masked(keep, tile):
    return jnp.where(keep, tile, 0.0)


def pairs_loop(g, width, body, first=0, last=PAIRS):
    def step(i, carry):
        for u in range(width):
            body(g * PAIRS + i * width + u)
        return carry

    lax.fori_loop(first // width, last // width, step, 0)


def forward_group(g, first, last, x, b, c, skip_ref, cd_ref, rows_ref, prod, turned, ssd, s_ref):
    cs = slice(g * N, (g + 1) * N)
    bg = b[:, cs]
    if first == 0:
        turned[...] = bg.astype(F32).T
        ri = lax.broadcasted_iota(jnp.int32, (Q, Q), 0)
        ci = lax.broadcasted_iota(jnp.int32, (Q, Q), 1)
        prod[...] = masked(ri >= ci, dot_t(c[:, cs], bg))
    low = low_lanes(Q)

    def body(p):
        at = lanes_at(p)
        cols = pair_cols(cd_ref, p)
        xp = x[:, at].astype(F32)
        xdt = (xp * pair_lanes(cols, H, low)).astype(BF16)
        tops, lows, states = [], [], []
        for e in (0, 1):
            col = cols[:, e : e + 1]
            row = rows_ref[2 * p + e]
            s00 = (prod[:128, :128] * jnp.exp(jnp.minimum(col[:128] - row[:, :128], 0.0))).astype(BF16)
            s10 = (prod[128:, :128] * jnp.exp(jnp.minimum(col[128:] - row[:, :128], 0.0))).astype(BF16)
            s11 = (prod[128:, 128:] * jnp.exp(jnp.minimum(col[128:] - row[:, 128:], 0.0))).astype(BF16)
            tops.append(dot(s00, xdt[:128]))
            lows.append(dot(jnp.concatenate([s10, s11], axis=1), xdt))
            bw = (turned[...] * jnp.exp(row[:, Q - 1 : Q] - row)).astype(BF16)
            states.append(dot(bw, xdt))
        skip = skip_ref[:, at]
        ssd[:128, at] = jnp.where(low[:128], tops[0], tops[1]) + skip * xp[:128]
        ssd[128:, at] = jnp.where(low[:128], lows[0], lows[1]) + skip * xp[128:]
        s_ref[g, p - g * PAIRS] = jnp.where(low[:N], states[0], states[1]).astype(BF16)

    pairs_loop(g, 2, body, first, last)


ROWS = 64


def rows_loop(body):
    def step(i, carry):
        body(pl.ds(pl.multiple_of(i * ROWS, ROWS), ROWS))
        return carry

    lax.fori_loop(0, Q // ROWS, step, 0)


def silu_of(z, at, gs):
    zf = z[at, gs].astype(F32)
    return 0.5 * zf * (1.0 + jnp.tanh(0.5 * zf))


def norm_group(g, z, c, inc, gain_ref, cd_ref, ssd, stat, normed, down, up_t, down_t, sa):
    gs = slice(g * GW, (g + 1) * GW)
    cg = c[:, g * N : (g + 1) * N]
    low = low_lanes(Q)

    def inter(p):
        at = lanes_at(p)
        cols = pair_cols(cd_ref, p)
        ssd[:, at] += jnp.exp(pair_lanes(cols, 0, low)) * dot(cg, inc[g, p - g * PAIRS])

    pairs_loop(g, 2, inter)
    gain = gain_ref[:, gs]

    def chunk(at):
        gated = ssd[at, gs] * silu_of(z, at, gs)
        rstd = lax.rsqrt(jnp.mean(gated * gated, axis=-1, keepdims=True) + EPS_NORM)
        hat = gated * rstd
        ssd[at, gs] = hat
        stat[g, at, :] = jnp.broadcast_to(rstd, (ROWS, 128))
        normed[at, :] = (hat * gain).astype(BF16)

    rows_loop(chunk)
    sa[:, gs] = SCALE * dot(up_t[...], normed[...])
    part = dot_t(down[:, gs], normed[...])
    if g == 0:
        down_t[...] = part
    else:
        down_t[...] += part


def gradient_group(g, z, c, wbuf, cot, down, up_row, gain_ref, rows_ref, ssd, stat, dn, turned, d, grad):
    gs = slice(g * GW, (g + 1) * GW)

    def column(i, carry):
        at = pl.ds(pl.multiple_of(i * 256, 256), 256)
        full = pl.ds(pl.multiple_of(g * GW + i * 256, 256), 256)
        w = wbuf[:, :, :, :, g, :, at].reshape(OUTF, 256)
        dn[:, at] = dot(cot[...], w) + SCALE * dot(up_row[...], down[:, full])
        return carry

    lax.fori_loop(0, GW // 256, column, 0)
    gain = gain_ref[:, gs]

    def chunk(at):
        hat = ssd[at, gs]
        wg = dn[at, :] * gain
        slope = jnp.mean(hat * wg, axis=-1, keepdims=True)
        d[at, gs] = (stat[g, at, 0:1] * (wg - hat * slope) * silu_of(z, at, gs)).astype(BF16)

    rows_loop(chunk)
    turned[...] = c[:, g * N : (g + 1) * N].astype(F32).T
    low_n = low_lanes(N)

    def body(p):
        dp = d[:, lanes_at(p)]
        halves = []
        for e in (0, 1):
            cw = (turned[...] * jnp.exp(rows_ref[2 * p + e])).astype(BF16)
            halves.append(dot(cw, dp))
        grad[g, p - g * PAIRS] = jnp.where(low_n, halves[0], halves[1]).astype(BF16)

    pairs_loop(g, 2, body)


def backward_group(g, b, c, d, outg, skip_ref, cd_ref, rows_ref, prod, o):
    cs = slice(g * N, (g + 1) * N)
    bg = b[:, cs]
    ri = lax.broadcasted_iota(jnp.int32, (Q, Q), 0)
    ci = lax.broadcasted_iota(jnp.int32, (Q, Q), 1)
    prod[...] = masked(ci >= ri, dot_t(bg, c[:, cs]))
    low = low_lanes(Q)

    def body(p):
        at = lanes_at(p)
        cols = pair_cols(cd_ref, p)
        dp = d[:, at]
        tops, lows = [], []
        for e in (0, 1):
            col = cols[:, e : e + 1]
            row = rows_ref[2 * p + e]
            s00 = (prod[:128, :128] * jnp.exp(jnp.minimum(row[:, :128] - col[:128], 0.0))).astype(BF16)
            s01 = (prod[:128, 128:] * jnp.exp(jnp.minimum(row[:, 128:] - col[:128], 0.0))).astype(BF16)
            s11 = (prod[128:, 128:] * jnp.exp(jnp.minimum(row[:, 128:] - col[128:], 0.0))).astype(BF16)
            tops.append(dot(jnp.concatenate([s00, s01], axis=1), dp))
            lows.append(dot(s11, dp[128:]))
        run = pair_lanes(cols, 0, low)
        cross = jnp.exp(run[Q - 1 : Q] - run) * dot(bg, outg[g, p - g * PAIRS])
        dt = pair_lanes(cols, H, low)
        skip = skip_ref[:, at]
        top = jnp.where(low[:128], tops[0], tops[1]) + cross[:128]
        bottom = jnp.where(low[:128], lows[0], lows[1]) + cross[128:]
        o[:128, at] = (dt[:128] * top + skip * dp[:128].astype(F32)).astype(BF16)
        o[128:, at] = (dt[128:] * bottom + skip * dp[128:].astype(F32)).astype(BF16)

    pairs_loop(g, 2, body)


SLOTS = 340
HALF = RANK // 2
VMEM_SCRATCH = [
    ("wbuf", (4, 4, 4, 2, G, 16, GW), BF16),
    ("x", (Q, INNER), BF16),
    ("z", (Q, INNER), BF16),
    ("b", (Q, G * N), BF16),
    ("c", (Q, G * N), BF16),
    ("cot", (Q, OUTF), BF16),
    ("down", (RANK, INNER), BF16),
    ("up", (RANK, OUTF), BF16),
    ("skip", (1, INNER), F32),
    ("cd", (Q, 128), F32),
    ("rows", (H, 1, Q), F32),
    ("tot", (G, PAIRS, 8, 128), F32),
    ("tots", (8, G, 8, 128), F32),
    ("prod", (Q, Q), F32),
    ("turned", (N, Q), F32),
    ("ssd", (Q, INNER), F32),
    ("stat", (G, Q, 128), F32),
    ("dn", (Q, GW), F32),
    ("normed", (Q, GW), BF16),
    ("d", (Q, INNER), BF16),
    ("o", (Q, INNER), BF16),
    ("up_t", (RANK, Q), BF16),
    ("up_row", (Q, RANK), BF16),
    ("down_t", (RANK, Q), F32),
    ("sa", (RANK, INNER), F32),
    ("sb", (RANK, OUTF), F32),
    ("s_own", (G, PAIRS, N, 128), BF16),
    ("s_got", (8, G, N, 128), BF16),
    ("s_made", (8, G, N, 128), BF16),
    ("s_out", (G, PAIRS, N, 128), BF16),
    ("g_own", (G, PAIRS, N, 128), BF16),
    ("g_got", (8, G, N, 128), BF16),
    ("g_made", (8, G, N, 128), BF16),
    ("g_out", (G, PAIRS, N, 128), BF16),
    ("a0", (HALF, INNER), F32),
    ("b0", (HALF, OUTF), F32),
    ("a0n", (HALF, INNER), BF16),
    ("b0n", (HALF, OUTF), BF16),
    ("a1", (HALF, 1024), F32),
    ("b1", (HALF, 512), F32),
    ("ra1", (3, HALF, 1024), BF16),
    ("rb1", (3, HALF, 512), BF16),
    ("a2", (RANK, 256), F32),
    ("b2", (RANK, 128), F32),
    ("ra2", (3, HALF, 256), F32),
    ("rb2", (3, HALF, 128), F32),
    ("ra3", (3, HALF, 256), F32),
    ("rb3", (3, HALF, 128), F32),
    ("sq", (3, 8, 128), F32),
    ("rsq", (2, 3, 8, 128), F32),
]
SUM_BUFS = (
    "a0", "b0", "a0n", "b0n", "a1", "b1", "ra1", "rb1", "a2", "b2", "ra2", "rb2", "ra3", "rb3", "sq", "rsq",
)
LOADS = ("x", "b", "c", "cot", "up", "z", "down")


def body(*refs):
    names = (
        "dtu", "bias", "alog", "skip_in", "gain", "w", "x", "b", "c", "cot", "up", "z", "down", "o_hbm", "da", "db",
    )
    r = dict(zip([n + "_in" if n in LOADS else n for n in names], refs))
    rest = refs[len(names) :]
    r.update(zip([n for n, _, _ in VMEM_SCRATCH], rest))
    send_sem, recv_sem, load_sem, own_sem, out_sem = rest[len(VMEM_SCRATCH) :]
    place = Place()
    lines = [place.along(axis, step) for axis in "yz" for step in (1, 2, 3)]

    everyone = greet(lines + [{"dp": place.dp, "ctx": place.position(o)} for o in range(1, 8)])
    own = []
    for g in range(G):
        copy = pltpu.make_async_copy(
            r["w"].at[:, pl.ds(g * GW, GW)],
            r["wbuf"].at[place.y, place.z, place.x, place.c, g],
            own_sem.at[g],
        )
        copy.start()
        own.append(copy)
    loads = {}
    for i, name in enumerate(LOADS):
        loads[name] = pltpu.make_async_copy(r[name + "_in"], r[name], load_sem.at[i])
        loads[name].start()
    link = Link(send_sem, recv_sem)
    weight = Weight(place, link, r["wbuf"])
    fwd = Exchange(place, link, r["s_own"], r["tots"], r["s_got"], r["s_made"], r["s_out"], False)
    bwd = Exchange(place, link, r["g_own"], r["tots"], r["g_got"], r["g_made"], r["g_out"], True)
    sums = Sums(place, link, r["sa"], r["sb"], r["da"], r["db"], [r[n] for n in SUM_BUFS]).steps()

    for copy in own:
        copy.wait()
    everyone()
    weight.step()
    decay_tables(
        r["dtu"], r["bias"], r["alog"], r["skip_in"], r["cd"], r["rows"], r["tot"], r["skip"]
    )
    me = place.ctx
    totals = []
    for o in range(1, 8):
        k = place.position(o)
        totals.append(link.push(r["tot"].at[:, k], r["tots"].at[me], {"dp": place.dp, "ctx": k}))
    r["tots"][me] = r["tot"][:, me]
    for name in ("x", "b", "c"):
        loads[name].wait()

    def forward(g):
        for first, last in ((0, PAIRS // 2), (PAIRS // 2, PAIRS)):
            forward_group(
                g, first, last, r["x"], r["b"], r["c"], r["skip"], r["cd"], r["rows"], r["prod"], r["turned"],
                r["ssd"], r["s_own"],
            )
            if last == PAIRS:
                fwd.scatter(g)
            if weight.at < 7:
                weight.step()

    def norm(g):
        fwd.finish(g)
        norm_group(
            g, r["z"], r["c"], r["s_out"], r["gain"], r["cd"], r["ssd"], r["stat"], r["normed"], r["down"],
            r["up_t"], r["down_t"], r["sa"],
        )

    def gradient(g):
        weight.ready(g)
        gradient_group(
            g, r["z"], r["c"], r["wbuf"], r["cot"], r["down"], r["up_row"], r["gain"], r["rows"], r["ssd"],
            r["stat"], r["dn"], r["turned"], r["d"], r["g_own"],
        )
        bwd.scatter(g)

    results = []

    def backward(g):
        bwd.finish(g)
        backward_group(
            g, r["b"], r["c"], r["d"], r["g_out"], r["skip"], r["cd"], r["rows"], r["prod"], r["o"]
        )
        at = pl.ds(g * GW, GW)
        copy = pltpu.make_async_copy(r["o"].at[:, at], r["o_hbm"].at[:, at], out_sem.at[g])
        copy.start()
        results.append(copy)

    forward(0)
    forward(1)
    for copy in totals:
        copy.wait_recv()
    forward(2)
    fwd.combine(0)
    forward(3)
    fwd.combine(1)
    weight.step()
    for name in ("cot", "up", "z", "down"):
        loads[name].wait()
    r["up_t"][...] = dot_t(r["up"][...], r["cot"][...]).astype(BF16)
    r["up_row"][...] = dot_t(r["cot"][...], r["up"][...]).astype(BF16)
    fwd.combine(2)
    norm(0)
    weight.step()
    fwd.combine(3)
    norm(1)
    norm(2)
    weight.step()
    norm(3)
    r["sb"][...] = SCALE * dot(r["down_t"][...].astype(BF16), r["cot"][...])
    next(sums)
    gradient(0)
    weight.step()
    next(sums)
    gradient(1)
    weight.step()
    bwd.combine(0)
    next(sums)
    gradient(2)
    bwd.combine(1)
    next(sums)
    gradient(3)
    bwd.combine(2)
    next(sums)
    backward(0)
    next(sums)
    bwd.combine(3)
    backward(1)
    next(sums)
    backward(2)
    next(sums)
    backward(3)
    for copy in results:
        copy.wait()
    link.drain()


def run_all(dtu, bias, alog, skip, gain, w, x, b, c, cot, up, z, down):
    vmem = pl.BlockSpec(memory_space=pltpu.VMEM)
    hbm = pl.BlockSpec(memory_space=pl.ANY)
    return pl.pallas_call(
        body,
        in_specs=[vmem] * 5 + [hbm] * 8,
        out_specs=[hbm, vmem, vmem],
        out_shape=[
            jax.ShapeDtypeStruct((Q, INNER), BF16),
            jax.ShapeDtypeStruct((32, RANK), F32),
            jax.ShapeDtypeStruct((16, RANK), F32),
        ],
        scratch_shapes=[pltpu.VMEM(shape, dtype) for _, shape, dtype in VMEM_SCRATCH]
        + [
            pltpu.SemaphoreType.DMA((SLOTS,)),
            pltpu.SemaphoreType.DMA((SLOTS,)),
            pltpu.SemaphoreType.DMA((len(LOADS),)),
            pltpu.SemaphoreType.DMA((G,)),
            pltpu.SemaphoreType.DMA((G,)),
        ],
        compiler_params=pltpu.CompilerParams(
            collective_id=1, has_side_effects=True, vmem_limit_bytes=VMEM_LIMIT
        ),
        name="whole_step",
    )(dtu, bias, alog, skip, gain, w, x, b, c, cot, up, z, down)


def on_device(x, z, b, c, dtu, bias, alog, skip, gain, down, up, w, cot):
    dx, da, db = run_all(
        dtu.T,
        bias.reshape(1, H),
        alog.reshape(1, H),
        skip.reshape(1, H),
        gain.reshape(1, INNER),
        w,
        x,
        b,
        c,
        cot,
        up,
        z,
        down,
    )
    return dx, da.T, db.T


def solution(mesh):
    rows = P(("dp", "ctx"), None)
    placed = (rows,) * 5 + (P(),) * 6 + (rows, rows)
    return jax.shard_map(
        on_device,
        mesh=mesh,
        in_specs=placed,
        out_specs=(rows, P(None, ("dp", "ctx")), P(None, ("dp", "ctx"))),
        check_vma=False,
    )
```

```python
import jax
import jax.numpy as jnp
from jax import lax
from jax.experimental import pallas as pl
from jax.experimental.pallas import tpu as pltpu
from jax.sharding import PartitionSpec as P

H = 64
P_SIZE = 64
N = 128
G = 4
Q = 256
INNER = 4096
OUTF = 2048
RANK = 64
GW = INNER // G
HG = H // G
PAIRS = HG // 2
EPS_NORM = 1e-05
CLIP_EPSILON = 1e-06
SCALE = 2.0
MESH = pl.DeviceIdType.MESH
F32 = jnp.float32
BF16 = jnp.bfloat16
VMEM_LIMIT = 56 * 1024 * 1024


def dot(a, b):
    return lax.dot_general(a, b, (((1,), (0,)), ((), ())), preferred_element_type=F32)


def dot_t(a, b):
    return lax.dot_general(a, b, (((1,), (1,)), ((), ())), preferred_element_type=F32)


def low_lanes(rows):
    return lax.broadcasted_iota(jnp.int32, (rows, 128), 1) < 64


def pair_cols(cd_ref, p):
    return pltpu.roll(cd_ref[...], lax.rem(128 - 2 * p, 128), 1)


def pair_lanes(cols, at, low):
    return jnp.where(low, cols[:, at : at + 1], cols[:, at + 1 : at + 2])


def lanes_at(p):
    return pl.ds(pl.multiple_of(p * 128, 128), 128)


class Place:
    def __init__(self):
        self.dp = lax.axis_index("dp")
        self.ctx = lax.axis_index("ctx")
        self.y = lax.div(self.dp, 4)
        self.z = lax.rem(self.dp, 4)
        self.x = lax.div(self.ctx, 2)
        self.c = lax.rem(self.ctx, 2)

    def coord(self, axis):
        return {"x": self.x, "y": self.y, "z": self.z}[axis]

    def along(self, axis, step):
        if axis == "x":
            return {"dp": self.dp, "ctx": lax.rem(self.x + step, 4) * 2 + self.c}
        if axis == "y":
            return {"dp": lax.rem(self.y + step, 4) * 4 + self.z, "ctx": self.ctx}
        return {"dp": self.y * 4 + lax.rem(self.z + step, 4), "ctx": self.ctx}

    def partner(self):
        return {"dp": self.dp, "ctx": self.x * 2 + 1 - self.c}

    def position(self, step):
        return lax.rem(self.ctx + step, 8)


def greet(devices):
    barrier = pltpu.get_barrier_semaphore()
    for device in devices:
        pl.semaphore_signal(barrier, inc=1, device_id=device, device_id_type=MESH)
    return lambda: pl.semaphore_wait(barrier, len(devices))


class Link:
    def __init__(self, send_sem, recv_sem):
        self.send_sem, self.recv_sem, self.used, self.sent = send_sem, recv_sem, 0, []

    def push(self, src, dst, device):
        copy = pltpu.make_async_remote_copy(
            src_ref=src,
            dst_ref=dst,
            send_sem=self.send_sem.at[self.used],
            recv_sem=self.recv_sem.at[self.used],
            device_id=device,
            device_id_type=MESH,
        )
        self.used += 1
        copy.start()
        self.sent.append(copy)
        return copy

    def settle(self, copies):
        for copy in copies:
            copy.wait_send()
        self.sent = [old for old in self.sent if all(old is not copy for copy in copies)]

    def drain(self):
        for copy in self.sent:
            copy.wait_send()


class Exchange:
    def __init__(self, place, link, own, tots, got, made, out, reverse):
        self.place, self.link, self.own, self.tots = place, link, own, tots
        self.got, self.made, self.out, self.reverse = got, made, out, reverse
        self.first, self.second = {}, {}

    def peer(self, k):
        return {"dp": self.place.dp, "ctx": k}

    def scatter(self, g):
        me = self.place.ctx
        self.first[g] = []
        for o in range(1, 8):
            k = self.place.position(o)
            self.first[g].append(self.link.push(self.own.at[g, k], self.got.at[me, g], self.peer(k)))
        self.got[me, g] = self.own[g, me]

    def combine(self, g):
        for copy in self.first[g]:
            copy.wait_recv()
        run = jnp.zeros((N, 128), F32)
        for j in range(7, -1, -1) if self.reverse else range(8):
            self.made[j, g] = run.astype(BF16)
            run = jnp.exp(self.tots[j, g, 0:1]) * run + self.got[j, g].astype(F32)
        me = self.place.ctx
        self.second[g] = []
        for o in range(1, 8):
            j = self.place.position(o)
            self.second[g].append(self.link.push(self.made.at[j, g], self.out.at[g, me], self.peer(j)))
        self.out[g, me] = self.made[me, g]

    def finish(self, g):
        for copy in self.second[g]:
            copy.wait_recv()


ORDERS = (("x", "y", "z"), ("y", "z", "x"), ("x", "z", "y"))
TILES = ((4, 1, 3), (3, 1, 4), (3, 2, 3), (3, 2, 3))


class Part:
    def __init__(self, place, link, buf, index):
        self.place, self.link, self.buf = place, link, buf
        self.order = ORDERS[index]
        self.start = [sum(tiles[:index]) for tiles in TILES]
        self.tiles = [tiles[index] for tiles in TILES]
        self.near, self.far = {}, {}

    def view(self, stage, step, g, tiles=None):
        picks = {}
        for i, axis in enumerate(self.order):
            if i < stage:
                picks[axis] = slice(None)
            elif i == stage:
                picks[axis] = lax.rem(self.place.coord(axis) + step, 4)
            else:
                picks[axis] = self.place.coord(axis)
        lo, count = (0, self.tiles[g]) if tiles is None else tiles
        return self.buf.at[
            picks["y"],
            picks["z"],
            picks["x"],
            self.place.c,
            g,
            slice(None),
            pl.ds((self.start[g] + lo) * 128, count * 128),
        ]

    def push(self, view, device):
        return self.link.push(view, view, device)

    def direct(self, stage, g):
        axis = self.order[stage]
        view = self.view(stage, 0, g)
        self.far[stage, g] = [self.push(view, self.place.along(axis, o)) for o in (1, 3, 2)]

    def hop_one(self, stage, g):
        axis = self.order[stage]
        view = self.view(stage, 0, g)
        self.near[stage, g] = (
            self.push(view, self.place.along(axis, 1)),
            self.push(view, self.place.along(axis, 3)),
        )

    def hop_two(self, stage, g):
        axis = self.order[stage]
        count = self.tiles[g]
        lo = (count + 1 - g % 2) // 2
        left, right = self.near[stage, g]
        self.far[stage, g] = []
        left.wait_recv()
        if lo:
            self.far[stage, g].append(self.push(self.view(stage, 3, g, (0, lo)), self.place.along(axis, 1)))
        right.wait_recv()
        if lo < count:
            self.far[stage, g].append(
                self.push(self.view(stage, 1, g, (lo, count - lo)), self.place.along(axis, 3))
            )

    def arrive(self, stage, g):
        for copy in self.far[stage, g]:
            copy.wait_recv()

    def share(self, step, g):
        return self.push(self.view(2, step, g), self.place.partner())


class Weight:
    def __init__(self, place, link, buf):
        self.parts = [Part(place, link, buf, i) for i in range(3)]
        self.shared = {g: [] for g in range(G)}

    def first(self, g):
        for part in self.parts:
            part.direct(0, g)

    def jump(self, g):
        for part in self.parts:
            part.arrive(0, g)
            part.direct(1, g)

    def one(self, g):
        for part in self.parts:
            part.arrive(0, g)
            part.hop_one(1, g)

    def two(self, g):
        for part in self.parts:
            part.hop_two(1, g)

    def last(self, g):
        for part in self.parts:
            part.arrive(1, g)
            part.hop_one(2, g)
        for part in self.parts:
            self.shared[g].append(part.share(0, g))

    def relay(self, g):
        for part in self.parts:
            part.hop_two(2, g)
        for part in self.parts:
            self.shared[g].append(part.share(3, g))
            self.shared[g].append(part.share(1, g))

    def land(self, g):
        for part in self.parts:
            part.arrive(2, g)
            self.shared[g].append(part.share(2, g))

    def ready(self, g):
        for copy in self.shared[g]:
            copy.wait_recv()


class Sums:
    def __init__(self, place, link, sa, sb, da, db, bufs):
        self.place, self.link, self.sa, self.sb, self.da, self.db = place, link, sa, sb, da, db
        self.bufs = bufs

    def spread(self, axis, wide, narrow, a, b, ra, rb):
        copies = []
        for o in (1, 2, 3):
            to = lax.rem(self.place.coord(axis) + o, 4)
            device = self.place.along(axis, o)
            ca = pl.ds(pl.multiple_of(to * wide, 128), wide)
            cb = pl.ds(pl.multiple_of(to * narrow, 128), narrow)
            copies.append(self.link.push(a.at[:, ca], ra.at[o - 1], device))
            copies.append(self.link.push(b.at[:, cb], rb.at[o - 1], device))
        return copies

    def summed(self, axis, wide, narrow, a, b, ra, rb):
        own = self.place.coord(axis)
        ca = pl.ds(pl.multiple_of(own * wide, 128), wide)
        cb = pl.ds(pl.multiple_of(own * narrow, 128), narrow)
        return (
            a[:, ca] + (ra[0].astype(F32) + ra[1].astype(F32) + ra[2].astype(F32)),
            b[:, cb] + (rb[0].astype(F32) + rb[1].astype(F32) + rb[2].astype(F32)),
        )

    def steps(self):
        place, push = self.place, self.link.push
        a0, b0, a0n, b0n, a1, b1, ra1, rb1, a2, b2, ra2, rb2, ra3, rb3, sq, rsq = self.bufs
        half = RANK // 2
        mine = pl.ds(pl.multiple_of(place.c * half, half), half)
        theirs = pl.ds(pl.multiple_of((1 - place.c) * half, half), half)
        partner = place.partner()

        def arrived(copies):
            for copy in copies:
                copy.wait_recv()

        copies = [push(self.sa.at[theirs], a0, partner), push(self.sb.at[theirs], b0, partner)]
        yield
        arrived(copies)
        a0[...] += self.sa[mine]
        b0[...] += self.sb[mine]
        a0n[...] = a0[...].astype(BF16)
        b0n[...] = b0[...].astype(BF16)
        copies = self.spread("y", 1024, 512, a0n, b0n, ra1, rb1)
        yield
        arrived(copies)
        a1[...], b1[...] = self.summed("y", 1024, 512, a0, b0, ra1, rb1)
        copies = self.spread("z", 256, 128, a1, b1, ra2, rb2)
        yield
        arrived(copies)
        a2[mine], b2[mine] = self.summed("z", 256, 128, a1, b1, ra2, rb2)
        copies = []
        for o in (1, 2, 3):
            device = place.along("x", o)
            copies.append(push(a2.at[mine], ra3.at[o - 1], device))
            copies.append(push(b2.at[mine], rb3.at[o - 1], device))
        yield
        arrived(copies)
        self.link.settle(copies)
        a2[mine] += ra3[0] + ra3[1] + ra3[2]
        b2[mine] += rb3[0] + rb3[1] + rb3[2]
        copies = [push(a2.at[mine], a2.at[mine], partner), push(b2.at[mine], b2.at[mine], partner)]
        yield
        arrived(copies)
        a = a2[...]
        b = b2[...]
        row = lax.broadcasted_iota(jnp.int32, (8, 128), 0)
        sq[0] = jnp.where(row == 0, jnp.sum(a * a), jnp.sum(b * b))
        for i, axis in enumerate("yz"):
            copies = [push(sq.at[i], rsq.at[i, o - 1], place.along(axis, o)) for o in (1, 2, 3)]
            yield
            arrived(copies)
            sq[i + 1] = sq[i] + (rsq[i, 0] + rsq[i, 1] + rsq[i, 2])
        total = sq[2]
        root_a = jnp.sqrt(total[0:1, 0:1] / (RANK * INNER) + CLIP_EPSILON)
        root_b = jnp.sqrt(total[1:2, 0:1] / (RANK * OUTF) + CLIP_EPSILON)
        a = jnp.where(place.ctx >= 4, a2[:, 128:], a2[:, :128]) / jnp.maximum(1.0, root_a)
        b = b2[...] / jnp.maximum(1.0, root_b)
        a = pltpu.roll(a, lax.rem(256 - 32 * place.ctx, 128), 1)
        b = pltpu.roll(b, lax.rem(128 - 16 * place.ctx, 128), 1)
        self.da[...] = a.T[:32, :]
        self.db[...] = b.T[:16, :]
        yield


def decay_tables(dtu_ref, bias_ref, alog_ref, skip_in, cd_ref, rows_ref, tot_ref, skip_ref):
    step = jax.nn.softplus(dtu_ref[...].T + bias_ref[...])
    run = -jnp.exp(alog_ref[...]) * step
    rows = lax.broadcasted_iota(jnp.int32, (Q, H), 0)
    shift = 1
    while shift < Q:
        run = run + jnp.where(rows >= shift, pltpu.roll(run, shift, 0), 0.0)
        shift *= 2
    both = jnp.concatenate([run, step], axis=1)
    cd_ref[...] = both
    turned = both.T
    for h in range(H):
        rows_ref[h] = turned[h : h + 1, :]
    low = low_lanes(8)
    last = both[Q - 1 : Q, :]
    for p in range(H // 2):
        pair = jnp.where(low, last[:, 2 * p : 2 * p + 1], last[:, 2 * p + 1 : 2 * p + 2])
        tot_ref[p // PAIRS, p % PAIRS] = pair
        skip = skip_in[...]
        skip_ref[:, p * 128 : (p + 1) * 128] = jnp.where(
            low[:1], skip[:, 2 * p : 2 * p + 1], skip[:, 2 * p + 1 : 2 * p + 2]
        )


def masked(keep, tile):
    return jnp.where(keep, tile, 0.0)


def pairs_loop(g, width, body, first=0, last=PAIRS):
    def step(i, carry):
        for u in range(width):
            body(g * PAIRS + i * width + u)
        return carry

    lax.fori_loop(first // width, last // width, step, 0)


def forward_group(g, first, last, x, b, c, skip_ref, cd_ref, rows_ref, prod, turned, ssd, s_ref):
    cs = slice(g * N, (g + 1) * N)
    bg = b[:, cs]
    if first == 0:
        turned[...] = bg.astype(F32).T
        ri = lax.broadcasted_iota(jnp.int32, (Q, Q), 0)
        ci = lax.broadcasted_iota(jnp.int32, (Q, Q), 1)
        prod[...] = masked(ri >= ci, dot_t(c[:, cs], bg))
    low = low_lanes(Q)

    def body(p):
        at = lanes_at(p)
        cols = pair_cols(cd_ref, p)
        xp = x[:, at].astype(F32)
        xdt = (xp * pair_lanes(cols, H, low)).astype(BF16)
        tops, lows, states = [], [], []
        for e in (0, 1):
            col = cols[:, e : e + 1]
            row = rows_ref[2 * p + e]
            s00 = (prod[:128, :128] * jnp.exp(jnp.minimum(col[:128] - row[:, :128], 0.0))).astype(BF16)
            s10 = (prod[128:, :128] * jnp.exp(jnp.minimum(col[128:] - row[:, :128], 0.0))).astype(BF16)
            s11 = (prod[128:, 128:] * jnp.exp(jnp.minimum(col[128:] - row[:, 128:], 0.0))).astype(BF16)
            tops.append(dot(s00, xdt[:128]))
            lows.append(dot(jnp.concatenate([s10, s11], axis=1), xdt))
            bw = (turned[...] * jnp.exp(row[:, Q - 1 : Q] - row)).astype(BF16)
            states.append(dot(bw, xdt))
        skip = skip_ref[:, at]
        ssd[:128, at] = jnp.where(low[:128], tops[0], tops[1]) + skip * xp[:128]
        ssd[128:, at] = jnp.where(low[:128], lows[0], lows[1]) + skip * xp[128:]
        s_ref[g, p - g * PAIRS] = jnp.where(low[:N], states[0], states[1]).astype(BF16)

    pairs_loop(g, 2, body, first, last)


ROWS = 64


def rows_loop(body):
    def step(i, carry):
        body(pl.ds(pl.multiple_of(i * ROWS, ROWS), ROWS))
        return carry

    lax.fori_loop(0, Q // ROWS, step, 0)


def silu_of(z, at, gs):
    zf = z[at, gs].astype(F32)
    return 0.5 * zf * (1.0 + jnp.tanh(0.5 * zf))


def norm_group(g, z, c, inc, gain_ref, cd_ref, ssd, stat, normed, down, up_t, down_t, sa):
    gs = slice(g * GW, (g + 1) * GW)
    cg = c[:, g * N : (g + 1) * N]
    low = low_lanes(Q)

    def inter(p):
        at = lanes_at(p)
        cols = pair_cols(cd_ref, p)
        ssd[:, at] += jnp.exp(pair_lanes(cols, 0, low)) * dot(cg, inc[g, p - g * PAIRS])

    pairs_loop(g, 2, inter)
    gain = gain_ref[:, gs]

    def chunk(at):
        gated = ssd[at, gs] * silu_of(z, at, gs)
        rstd = lax.rsqrt(jnp.mean(gated * gated, axis=-1, keepdims=True) + EPS_NORM)
        hat = gated * rstd
        ssd[at, gs] = hat
        stat[g, at, :] = jnp.broadcast_to(rstd, (ROWS, 128))
        normed[at, :] = (hat * gain).astype(BF16)

    rows_loop(chunk)
    sa[:, gs] = SCALE * dot(up_t[...], normed[...])
    part = dot_t(down[:, gs], normed[...])
    if g == 0:
        down_t[...] = part
    else:
        down_t[...] += part


def project_group(g, wbuf, cot, down, up_row, dn):

    def column(i, carry):
        at = pl.ds(pl.multiple_of(i * 256, 256), 256)
        full = pl.ds(pl.multiple_of(g * GW + i * 256, 256), 256)
        w = wbuf[:, :, :, :, g, :, at].reshape(OUTF, 256)
        dn[:, at] = dot(cot[...], w) + SCALE * dot(up_row[...], down[:, full])
        return carry

    lax.fori_loop(0, GW // 256, column, 0)


def gradient_group(g, z, c, gain_ref, rows_ref, ssd, stat, dn, turned, d, grad):
    gs = slice(g * GW, (g + 1) * GW)
    gain = gain_ref[:, gs]

    def chunk(at):
        hat = ssd[at, gs]
        wg = dn[at, :] * gain
        slope = jnp.mean(hat * wg, axis=-1, keepdims=True)
        d[at, gs] = (stat[g, at, 0:1] * (wg - hat * slope) * silu_of(z, at, gs)).astype(BF16)

    rows_loop(chunk)
    turned[...] = c[:, g * N : (g + 1) * N].astype(F32).T
    low_n = low_lanes(N)

    def body(p):
        dp = d[:, lanes_at(p)]
        halves = []
        for e in (0, 1):
            cw = (turned[...] * jnp.exp(rows_ref[2 * p + e])).astype(BF16)
            halves.append(dot(cw, dp))
        grad[g, p - g * PAIRS] = jnp.where(low_n, halves[0], halves[1]).astype(BF16)

    pairs_loop(g, 2, body)


def backward_group(g, b, c, d, outg, skip_ref, cd_ref, rows_ref, prod, o):
    cs = slice(g * N, (g + 1) * N)
    bg = b[:, cs]
    ri = lax.broadcasted_iota(jnp.int32, (Q, Q), 0)
    ci = lax.broadcasted_iota(jnp.int32, (Q, Q), 1)
    prod[...] = masked(ci >= ri, dot_t(bg, c[:, cs]))
    low = low_lanes(Q)

    def body(p):
        at = lanes_at(p)
        cols = pair_cols(cd_ref, p)
        dp = d[:, at]
        tops, lows = [], []
        for e in (0, 1):
            col = cols[:, e : e + 1]
            row = rows_ref[2 * p + e]
            s00 = (prod[:128, :128] * jnp.exp(jnp.minimum(row[:, :128] - col[:128], 0.0))).astype(BF16)
            s01 = (prod[:128, 128:] * jnp.exp(jnp.minimum(row[:, 128:] - col[:128], 0.0))).astype(BF16)
            s11 = (prod[128:, 128:] * jnp.exp(jnp.minimum(row[:, 128:] - col[128:], 0.0))).astype(BF16)
            tops.append(dot(jnp.concatenate([s00, s01], axis=1), dp))
            lows.append(dot(s11, dp[128:]))
        run = pair_lanes(cols, 0, low)
        cross = jnp.exp(run[Q - 1 : Q] - run) * dot(bg, outg[g, p - g * PAIRS])
        dt = pair_lanes(cols, H, low)
        skip = skip_ref[:, at]
        top = jnp.where(low[:128], tops[0], tops[1]) + cross[:128]
        bottom = jnp.where(low[:128], lows[0], lows[1]) + cross[128:]
        o[:128, at] = (dt[:128] * top + skip * dp[:128].astype(F32)).astype(BF16)
        o[128:, at] = (dt[128:] * bottom + skip * dp[128:].astype(F32)).astype(BF16)

    pairs_loop(g, 2, body)


SLOTS = 350
HALF = RANK // 2
VMEM_SCRATCH = [
    ("wbuf", (4, 4, 4, 2, G, 16, GW), BF16),
    ("x", (Q, INNER), BF16),
    ("z", (Q, INNER), BF16),
    ("b", (Q, G * N), BF16),
    ("c", (Q, G * N), BF16),
    ("cot", (Q, OUTF), BF16),
    ("down", (RANK, INNER), BF16),
    ("up", (RANK, OUTF), BF16),
    ("skip", (1, INNER), F32),
    ("cd", (Q, 128), F32),
    ("rows", (H, 1, Q), F32),
    ("tot", (G, PAIRS, 8, 128), F32),
    ("tots", (8, G, 8, 128), F32),
    ("prod", (Q, Q), F32),
    ("turned", (N, Q), F32),
    ("ssd", (Q, INNER), F32),
    ("stat", (G, Q, 128), F32),
    ("dn", (Q, GW), F32),
    ("normed", (Q, GW), BF16),
    ("d", (Q, INNER), BF16),
    ("up_t", (RANK, Q), BF16),
    ("up_row", (Q, RANK), BF16),
    ("down_t", (RANK, Q), F32),
    ("sa", (RANK, INNER), F32),
    ("sb", (RANK, OUTF), F32),
    ("s_own", (G, PAIRS, N, 128), BF16),
    ("s_got", (8, G, N, 128), BF16),
    ("s_made", (8, G, N, 128), BF16),
    ("s_out", (G, PAIRS, N, 128), BF16),
    ("g_own", (G, PAIRS, N, 128), BF16),
    ("g_got", (8, G, N, 128), BF16),
    ("g_made", (8, G, N, 128), BF16),
    ("g_out", (G, PAIRS, N, 128), BF16),
    ("a0", (HALF, INNER), F32),
    ("b0", (HALF, OUTF), F32),
    ("a0n", (HALF, INNER), BF16),
    ("b0n", (HALF, OUTF), BF16),
    ("a1", (HALF, 1024), F32),
    ("b1", (HALF, 512), F32),
    ("ra1", (3, HALF, 1024), BF16),
    ("rb1", (3, HALF, 512), BF16),
    ("a2", (RANK, 256), F32),
    ("b2", (RANK, 128), F32),
    ("ra2", (3, HALF, 256), F32),
    ("rb2", (3, HALF, 128), F32),
    ("ra3", (3, HALF, 256), F32),
    ("rb3", (3, HALF, 128), F32),
    ("sq", (3, 8, 128), F32),
    ("rsq", (2, 3, 8, 128), F32),
]
SUM_BUFS = (
    "a0", "b0", "a0n", "b0n", "a1", "b1", "ra1", "rb1", "a2", "b2", "ra2", "rb2", "ra3", "rb3", "sq", "rsq",
)
LOADS = ("x", "b", "c", "cot", "up", "z", "down")


def body(*refs):
    names = (
        "dtu", "bias", "alog", "skip_in", "gain", "w", "x", "b", "c", "cot", "up", "z", "down", "o", "da", "db",
    )
    r = dict(zip([n + "_in" if n in LOADS else n for n in names], refs))
    rest = refs[len(names) :]
    r.update(zip([n for n, _, _ in VMEM_SCRATCH], rest))
    send_sem, recv_sem, load_sem, own_sem = rest[len(VMEM_SCRATCH) :]
    place = Place()
    lines = [place.along(axis, step) for axis in "yz" for step in (1, 2, 3)]

    everyone = greet(lines + [{"dp": place.dp, "ctx": place.position(o)} for o in range(1, 8)])
    own = []
    for g in range(G):
        copy = pltpu.make_async_copy(
            r["w"].at[:, pl.ds(g * GW, GW)],
            r["wbuf"].at[place.y, place.z, place.x, place.c, g],
            own_sem.at[g],
        )
        copy.start()
        own.append(copy)
    loads = {}
    for i, name in enumerate(LOADS):
        loads[name] = pltpu.make_async_copy(r[name + "_in"], r[name], load_sem.at[i])
        loads[name].start()
    link = Link(send_sem, recv_sem)
    weight = Weight(place, link, r["wbuf"])
    fwd = Exchange(place, link, r["s_own"], r["tots"], r["s_got"], r["s_made"], r["s_out"], False)
    bwd = Exchange(place, link, r["g_own"], r["tots"], r["g_got"], r["g_made"], r["g_out"], True)
    sums = Sums(place, link, r["sa"], r["sb"], r["da"], r["db"], [r[n] for n in SUM_BUFS]).steps()

    for copy in own:
        copy.wait()
    everyone()
    for g in range(G):
        weight.first(g)
    decay_tables(
        r["dtu"], r["bias"], r["alog"], r["skip_in"], r["cd"], r["rows"], r["tot"], r["skip"]
    )
    me = place.ctx
    totals = []
    for o in range(1, 8):
        k = place.position(o)
        totals.append(link.push(r["tot"].at[:, k], r["tots"].at[me], {"dp": place.dp, "ctx": k}))
    r["tots"][me] = r["tot"][:, me]
    for name in ("x", "b", "c"):
        loads[name].wait()

    def forward(g, half):
        forward_group(
            g, half * PAIRS // 2, (half + 1) * PAIRS // 2, r["x"], r["b"], r["c"], r["skip"], r["cd"], r["rows"],
            r["prod"], r["turned"], r["ssd"], r["s_own"],
        )
        if half:
            fwd.scatter(g)

    def total():
        for copy in totals:
            copy.wait_recv()

    def lora():
        for name in ("cot", "up", "z", "down"):
            loads[name].wait()
        r["up_t"][...] = dot_t(r["up"][...], r["cot"][...]).astype(BF16)
        r["up_row"][...] = dot_t(r["cot"][...], r["up"][...]).astype(BF16)

    def lora_sum():
        r["sb"][...] = SCALE * dot(r["down_t"][...].astype(BF16), r["cot"][...])

    def norm(g):
        fwd.finish(g)
        norm_group(
            g, r["z"], r["c"], r["s_out"], r["gain"], r["cd"], r["ssd"], r["stat"], r["normed"], r["down"],
            r["up_t"], r["down_t"], r["sa"],
        )

    def project(g):
        weight.ready(g)
        project_group(g, r["wbuf"], r["cot"], r["down"], r["up_row"], r["dn"])

    def gradient(g):
        gradient_group(
            g, r["z"], r["c"], r["gain"], r["rows"], r["ssd"], r["stat"], r["dn"], r["turned"], r["d"], r["g_own"]
        )
        bwd.scatter(g)


    def backward(g):
        bwd.finish(g)
        backward_group(
            g, r["b"], r["c"], r["d"], r["g_out"], r["skip"], r["cd"], r["rows"], r["prod"], r["o"]
        )

    forward(0, 0)
    forward(0, 1)
    forward(1, 0)
    weight.jump(0)
    weight.one(1)
    forward(1, 1)
    forward(2, 0)
    forward(2, 1)
    forward(3, 0)
    weight.last(0)
    weight.two(1)
    weight.one(2)
    forward(3, 1)
    total()
    fwd.combine(0)
    lora()
    weight.last(1)
    weight.two(2)
    weight.one(3)
    fwd.combine(1)
    fwd.combine(2)
    norm(0)
    weight.relay(0)
    weight.last(2)
    weight.two(3)
    fwd.combine(3)
    norm(1)
    weight.relay(1)
    weight.last(3)
    norm(2)
    weight.land(0)
    norm(3)
    lora_sum()
    next(sums)
    project(0)
    weight.relay(2)
    weight.land(1)
    gradient(0)
    project(1)
    weight.relay(3)
    next(sums)
    weight.land(2)
    gradient(1)
    bwd.combine(0)
    project(2)
    weight.land(3)
    gradient(2)
    bwd.combine(1)
    project(3)
    next(sums)
    gradient(3)
    bwd.combine(2)
    next(sums)
    backward(0)
    backward(1)
    next(sums)
    bwd.combine(3)
    next(sums)
    backward(2)
    next(sums)
    backward(3)
    next(sums)
    link.drain()


def run_all(dtu, bias, alog, skip, gain, w, x, b, c, cot, up, z, down):
    vmem = pl.BlockSpec(memory_space=pltpu.VMEM)
    hbm = pl.BlockSpec(memory_space=pl.ANY)
    return pl.pallas_call(
        body,
        in_specs=[vmem] * 5 + [hbm] * 8,
        out_specs=[vmem, vmem, vmem],
        out_shape=[
            pltpu.VMEM((Q, INNER), BF16),
            jax.ShapeDtypeStruct((32, RANK), F32),
            jax.ShapeDtypeStruct((16, RANK), F32),
        ],
        scratch_shapes=[pltpu.VMEM(shape, dtype) for _, shape, dtype in VMEM_SCRATCH]
        + [
            pltpu.SemaphoreType.DMA((SLOTS,)),
            pltpu.SemaphoreType.DMA((SLOTS,)),
            pltpu.SemaphoreType.DMA((len(LOADS),)),
            pltpu.SemaphoreType.DMA((G,)),
        ],
        compiler_params=pltpu.CompilerParams(
            collective_id=1, has_side_effects=True, vmem_limit_bytes=VMEM_LIMIT
        ),
        name="whole_step",
    )(dtu, bias, alog, skip, gain, w, x, b, c, cot, up, z, down)


def on_device(x, z, b, c, dtu, bias, alog, skip, gain, down, up, w, cot):
    dx, da, db = run_all(
        dtu.T,
        bias.reshape(1, H),
        alog.reshape(1, H),
        skip.reshape(1, H),
        gain.reshape(1, INNER),
        w,
        x,
        b,
        c,
        cot,
        up,
        z,
        down,
    )
    return dx, da.T, db.T


def solution(mesh):
    rows = P(("dp", "ctx"), None)
    placed = (rows,) * 5 + (P(),) * 6 + (rows, rows)
    return jax.shard_map(
        on_device,
        mesh=mesh,
        in_specs=placed,
        out_specs=(rows, P(None, ("dp", "ctx")), P(None, ("dp", "ctx"))),
        check_vma=False,
    )
```

```python
import jax
import jax.numpy as jnp
from jax import lax
from jax.experimental import pallas as pl
from jax.experimental.pallas import tpu as pltpu
from jax.sharding import PartitionSpec as P

H = 64
P_SIZE = 64
N = 128
G = 4
Q = 256
INNER = 4096
OUTF = 2048
RANK = 64
GW = INNER // G
HG = H // G
PAIRS = HG // 2
EPS_NORM = 1e-05
CLIP_EPSILON = 1e-06
SCALE = 2.0
MESH = pl.DeviceIdType.MESH
F32 = jnp.float32
BF16 = jnp.bfloat16
VMEM_LIMIT = 56 * 1024 * 1024


def dot(a, b):
    return lax.dot_general(a, b, (((1,), (0,)), ((), ())), preferred_element_type=F32)


def dot_t(a, b):
    return lax.dot_general(a, b, (((1,), (1,)), ((), ())), preferred_element_type=F32)


def low_lanes(rows):
    return lax.broadcasted_iota(jnp.int32, (rows, 128), 1) < 64


def pair_cols(cd_ref, p):
    return pltpu.roll(cd_ref[...], lax.rem(128 - 2 * p, 128), 1)


def pair_lanes(cols, at, low):
    return jnp.where(low, cols[:, at : at + 1], cols[:, at + 1 : at + 2])


def lanes_at(p):
    return pl.ds(pl.multiple_of(p * 128, 128), 128)


class Place:
    def __init__(self):
        self.dp = lax.axis_index("dp")
        self.ctx = lax.axis_index("ctx")
        self.y = lax.div(self.dp, 4)
        self.z = lax.rem(self.dp, 4)
        self.x = lax.div(self.ctx, 2)
        self.c = lax.rem(self.ctx, 2)

    def coord(self, axis):
        return {"x": self.x, "y": self.y, "z": self.z}[axis]

    def along(self, axis, step):
        if axis == "x":
            return {"dp": self.dp, "ctx": lax.rem(self.x + step, 4) * 2 + self.c}
        if axis == "y":
            return {"dp": lax.rem(self.y + step, 4) * 4 + self.z, "ctx": self.ctx}
        return {"dp": self.y * 4 + lax.rem(self.z + step, 4), "ctx": self.ctx}

    def partner(self):
        return {"dp": self.dp, "ctx": self.x * 2 + 1 - self.c}

    def position(self, step):
        return lax.rem(self.ctx + step, 8)


def greet(devices):
    barrier = pltpu.get_barrier_semaphore()
    for device in devices:
        pl.semaphore_signal(barrier, inc=1, device_id=device, device_id_type=MESH)
    return lambda: pl.semaphore_wait(barrier, len(devices))


class Link:
    def __init__(self, send_sem, recv_sem):
        self.send_sem, self.recv_sem, self.used, self.sent = send_sem, recv_sem, 0, []

    def push(self, src, dst, device):
        copy = pltpu.make_async_remote_copy(
            src_ref=src,
            dst_ref=dst,
            send_sem=self.send_sem.at[self.used],
            recv_sem=self.recv_sem.at[self.used],
            device_id=device,
            device_id_type=MESH,
        )
        self.used += 1
        copy.start()
        self.sent.append(copy)
        return copy

    def settle(self, copies):
        for copy in copies:
            copy.wait_send()
        self.sent = [old for old in self.sent if all(old is not copy for copy in copies)]

    def drain(self):
        for copy in self.sent:
            copy.wait_send()


class Exchange:
    def __init__(self, place, link, own, tots, got, made, out, reverse):
        self.place, self.link, self.own, self.tots = place, link, own, tots
        self.got, self.made, self.out, self.reverse = got, made, out, reverse
        self.first, self.second = {}, {}

    def peer(self, k):
        return {"dp": self.place.dp, "ctx": k}

    def scatter(self, g):
        me = self.place.ctx
        self.first[g] = []
        for o in range(1, 8):
            k = self.place.position(o)
            self.first[g].append(self.link.push(self.own.at[g, k], self.got.at[me, g], self.peer(k)))
        self.got[me, g] = self.own[g, me]

    def combine(self, g):
        for copy in self.first[g]:
            copy.wait_recv()
        run = jnp.zeros((N, 128), F32)
        for j in range(7, -1, -1) if self.reverse else range(8):
            self.made[j, g] = run.astype(BF16)
            run = jnp.exp(self.tots[j, g, 0:1]) * run + self.got[j, g].astype(F32)
        me = self.place.ctx
        self.second[g] = []
        for o in range(1, 8):
            j = self.place.position(o)
            self.second[g].append(self.link.push(self.made.at[j, g], self.out.at[g, me], self.peer(j)))
        self.out[g, me] = self.made[me, g]

    def finish(self, g):
        for copy in self.second[g]:
            copy.wait_recv()


ORDERS = (("x", "y", "z"), ("y", "z", "x"), ("x", "z", "y"))
TILES = ((4, 1, 3), (3, 1, 4), (3, 2, 3), (3, 2, 3))


class Part:
    def __init__(self, place, link, buf, index):
        self.place, self.link, self.buf = place, link, buf
        self.order = ORDERS[index]
        self.start = [sum(tiles[:index]) for tiles in TILES]
        self.tiles = [tiles[index] for tiles in TILES]
        self.near, self.far = {}, {}

    def view(self, stage, step, g, tiles=None):
        picks = {}
        for i, axis in enumerate(self.order):
            if i < stage:
                picks[axis] = slice(None)
            elif i == stage:
                picks[axis] = lax.rem(self.place.coord(axis) + step, 4)
            else:
                picks[axis] = self.place.coord(axis)
        lo, count = (0, self.tiles[g]) if tiles is None else tiles
        return self.buf.at[
            picks["y"],
            picks["z"],
            picks["x"],
            self.place.c,
            g,
            slice(None),
            pl.ds((self.start[g] + lo) * 128, count * 128),
        ]

    def push(self, view, device):
        return self.link.push(view, view, device)

    def direct(self, stage, g):
        axis = self.order[stage]
        view = self.view(stage, 0, g)
        self.far[stage, g] = [self.push(view, self.place.along(axis, o)) for o in (1, 3, 2)]

    def hop_one(self, stage, g):
        axis = self.order[stage]
        view = self.view(stage, 0, g)
        self.near[stage, g] = (
            self.push(view, self.place.along(axis, 1)),
            self.push(view, self.place.along(axis, 3)),
        )

    def hop_two(self, stage, g):
        axis = self.order[stage]
        count = self.tiles[g]
        lo = (count + 1 - g % 2) // 2
        left, right = self.near[stage, g]
        self.far[stage, g] = []
        left.wait_recv()
        if lo:
            self.far[stage, g].append(self.push(self.view(stage, 3, g, (0, lo)), self.place.along(axis, 1)))
        right.wait_recv()
        if lo < count:
            self.far[stage, g].append(
                self.push(self.view(stage, 1, g, (lo, count - lo)), self.place.along(axis, 3))
            )

    def arrive(self, stage, g):
        for copy in self.far[stage, g]:
            copy.wait_recv()

    def share(self, step, g):
        return self.push(self.view(2, step, g), self.place.partner())


class Weight:
    def __init__(self, place, link, buf):
        self.parts = [Part(place, link, buf, i) for i in range(3)]
        self.shared = {g: [] for g in range(G)}

    def first(self, g):
        for part in self.parts:
            part.direct(0, g)

    def jump(self, g):
        for part in self.parts:
            part.arrive(0, g)
            part.direct(1, g)

    def one(self, g):
        for part in self.parts:
            part.arrive(0, g)
            part.hop_one(1, g)

    def two(self, g):
        for part in self.parts:
            part.hop_two(1, g)

    def last(self, g):
        for part in self.parts:
            part.arrive(1, g)
            part.hop_one(2, g)
        for part in self.parts:
            self.shared[g].append(part.share(0, g))

    def relay(self, g):
        for part in self.parts:
            part.hop_two(2, g)
        for part in self.parts:
            self.shared[g].append(part.share(3, g))
            self.shared[g].append(part.share(1, g))

    def land(self, g):
        for part in self.parts:
            part.arrive(2, g)
            self.shared[g].append(part.share(2, g))

    def ready(self, g):
        for copy in self.shared[g]:
            copy.wait_recv()


class Sums:
    def __init__(self, place, link, sa, sb, da, db, bufs):
        self.place, self.link, self.sa, self.sb, self.da, self.db = place, link, sa, sb, da, db
        self.bufs = bufs

    def spread(self, axis, wide, narrow, a, b, ra, rb):
        copies = []
        for o in (1, 2, 3):
            to = lax.rem(self.place.coord(axis) + o, 4)
            device = self.place.along(axis, o)
            ca = pl.ds(pl.multiple_of(to * wide, 128), wide)
            cb = pl.ds(pl.multiple_of(to * narrow, 128), narrow)
            copies.append(self.link.push(a.at[:, ca], ra.at[o - 1], device))
            copies.append(self.link.push(b.at[:, cb], rb.at[o - 1], device))
        return copies

    def summed(self, axis, wide, narrow, a, b, ra, rb):
        own = self.place.coord(axis)
        ca = pl.ds(pl.multiple_of(own * wide, 128), wide)
        cb = pl.ds(pl.multiple_of(own * narrow, 128), narrow)
        return (
            a[:, ca] + (ra[0].astype(F32) + ra[1].astype(F32) + ra[2].astype(F32)),
            b[:, cb] + (rb[0].astype(F32) + rb[1].astype(F32) + rb[2].astype(F32)),
        )

    def steps(self):
        place, push = self.place, self.link.push
        a0, b0, a0n, b0n, a1, b1, ra1, rb1, a2, b2, ra2, rb2, ra3, rb3, sq, rsq = self.bufs
        half = RANK // 2
        mine = pl.ds(pl.multiple_of(place.c * half, half), half)
        theirs = pl.ds(pl.multiple_of((1 - place.c) * half, half), half)
        partner = place.partner()

        def arrived(copies):
            for copy in copies:
                copy.wait_recv()

        copies = [push(self.sa.at[theirs], a0, partner), push(self.sb.at[theirs], b0, partner)]
        yield
        arrived(copies)
        a0[...] += self.sa[mine]
        b0[...] += self.sb[mine]
        a0n[...] = a0[...].astype(BF16)
        b0n[...] = b0[...].astype(BF16)
        copies = self.spread("y", 1024, 512, a0n, b0n, ra1, rb1)
        yield
        arrived(copies)
        a1[...], b1[...] = self.summed("y", 1024, 512, a0, b0, ra1, rb1)
        copies = self.spread("z", 256, 128, a1, b1, ra2, rb2)
        yield
        arrived(copies)
        a2[mine], b2[mine] = self.summed("z", 256, 128, a1, b1, ra2, rb2)
        copies = []
        for o in (1, 2, 3):
            device = place.along("x", o)
            copies.append(push(a2.at[mine], ra3.at[o - 1], device))
            copies.append(push(b2.at[mine], rb3.at[o - 1], device))
        yield
        arrived(copies)
        self.link.settle(copies)
        a2[mine] += ra3[0] + ra3[1] + ra3[2]
        b2[mine] += rb3[0] + rb3[1] + rb3[2]
        copies = [push(a2.at[mine], a2.at[mine], partner), push(b2.at[mine], b2.at[mine], partner)]
        yield
        arrived(copies)
        a = a2[...]
        b = b2[...]
        row = lax.broadcasted_iota(jnp.int32, (8, 128), 0)
        sq[0] = jnp.where(row == 0, jnp.sum(a * a), jnp.sum(b * b))
        for i, axis in enumerate("yz"):
            copies = [push(sq.at[i], rsq.at[i, o - 1], place.along(axis, o)) for o in (1, 2, 3)]
            yield
            arrived(copies)
            sq[i + 1] = sq[i] + (rsq[i, 0] + rsq[i, 1] + rsq[i, 2])
        total = sq[2]
        root_a = jnp.sqrt(total[0:1, 0:1] / (RANK * INNER) + CLIP_EPSILON)
        root_b = jnp.sqrt(total[1:2, 0:1] / (RANK * OUTF) + CLIP_EPSILON)
        a = jnp.where(place.ctx >= 4, a2[:, 128:], a2[:, :128]) / jnp.maximum(1.0, root_a)
        b = b2[...] / jnp.maximum(1.0, root_b)
        a = pltpu.roll(a, lax.rem(256 - 32 * place.ctx, 128), 1)
        b = pltpu.roll(b, lax.rem(128 - 16 * place.ctx, 128), 1)
        self.da[...] = a.T[:32, :]
        self.db[...] = b.T[:16, :]
        yield


def decay_tables(dtu_ref, bias_ref, alog_ref, skip_in, cd_ref, rows_ref, tot_ref, skip_ref):
    step = jax.nn.softplus(dtu_ref[...].T + bias_ref[...])
    run = -jnp.exp(alog_ref[...]) * step
    rows = lax.broadcasted_iota(jnp.int32, (Q, H), 0)
    shift = 1
    while shift < Q:
        run = run + jnp.where(rows >= shift, pltpu.roll(run, shift, 0), 0.0)
        shift *= 2
    both = jnp.concatenate([run, step], axis=1)
    cd_ref[...] = both
    turned = both.T
    for h in range(H):
        rows_ref[h] = turned[h : h + 1, :]
    low = low_lanes(8)
    last = both[Q - 1 : Q, :]
    for p in range(H // 2):
        pair = jnp.where(low, last[:, 2 * p : 2 * p + 1], last[:, 2 * p + 1 : 2 * p + 2])
        tot_ref[p // PAIRS, p % PAIRS] = pair
        skip = skip_in[...]
        skip_ref[:, p * 128 : (p + 1) * 128] = jnp.where(
            low[:1], skip[:, 2 * p : 2 * p + 1], skip[:, 2 * p + 1 : 2 * p + 2]
        )


def masked(keep, tile):
    return jnp.where(keep, tile, 0.0)


def pairs_loop(g, width, body, first=0, last=PAIRS):
    def step(i, carry):
        for u in range(width):
            body(g * PAIRS + i * width + u)
        return carry

    lax.fori_loop(first // width, last // width, step, 0)


def forward_group(g, first, last, x, b, c, skip_ref, cd_ref, rows_ref, prod, turned, ssd, s_ref):
    cs = slice(g * N, (g + 1) * N)
    bg = b[:, cs]
    if first == 0:
        turned[...] = bg.astype(F32).T
        ri = lax.broadcasted_iota(jnp.int32, (Q, Q), 0)
        ci = lax.broadcasted_iota(jnp.int32, (Q, Q), 1)
        prod[...] = masked(ri >= ci, dot_t(c[:, cs], bg))
    low = low_lanes(Q)

    def body(p):
        at = lanes_at(p)
        cols = pair_cols(cd_ref, p)
        xp = x[:, at].astype(F32)
        xdt = (xp * pair_lanes(cols, H, low)).astype(BF16)
        tops, lows, states = [], [], []
        for e in (0, 1):
            col = cols[:, e : e + 1]
            row = rows_ref[2 * p + e]
            s00 = (prod[:128, :128] * jnp.exp(jnp.minimum(col[:128] - row[:, :128], 0.0))).astype(BF16)
            s10 = (prod[128:, :128] * jnp.exp(jnp.minimum(col[128:] - row[:, :128], 0.0))).astype(BF16)
            s11 = (prod[128:, 128:] * jnp.exp(jnp.minimum(col[128:] - row[:, 128:], 0.0))).astype(BF16)
            tops.append(dot(s00, xdt[:128]))
            lows.append(dot(jnp.concatenate([s10, s11], axis=1), xdt))
            bw = (turned[...] * jnp.exp(row[:, Q - 1 : Q] - row)).astype(BF16)
            states.append(dot(bw, xdt))
        skip = skip_ref[:, at]
        ssd[:128, at] = jnp.where(low[:128], tops[0], tops[1]) + skip * xp[:128]
        ssd[128:, at] = jnp.where(low[:128], lows[0], lows[1]) + skip * xp[128:]
        s_ref[g, p - g * PAIRS] = jnp.where(low[:N], states[0], states[1]).astype(BF16)

    pairs_loop(g, 2, body, first, last)


ROWS = 64


def rows_loop(body):
    def step(i, carry):
        body(pl.ds(pl.multiple_of(i * ROWS, ROWS), ROWS))
        return carry

    lax.fori_loop(0, Q // ROWS, step, 0)


def silu_of(z, at, gs):
    zf = z[at, gs].astype(F32)
    return 0.5 * zf * (1.0 + jnp.tanh(0.5 * zf))


def norm_group(g, z, c, inc, gain_ref, cd_ref, ssd, stat, normed, down, up_t, down_t, sa):
    gs = slice(g * GW, (g + 1) * GW)
    cg = c[:, g * N : (g + 1) * N]
    low = low_lanes(Q)

    def inter(p):
        at = lanes_at(p)
        cols = pair_cols(cd_ref, p)
        ssd[:, at] += jnp.exp(pair_lanes(cols, 0, low)) * dot(cg, inc[g, p - g * PAIRS])

    pairs_loop(g, 2, inter)
    gain = gain_ref[:, gs]

    def chunk(at):
        gated = ssd[at, gs] * silu_of(z, at, gs)
        rstd = lax.rsqrt(jnp.mean(gated * gated, axis=-1, keepdims=True) + EPS_NORM)
        hat = gated * rstd
        ssd[at, gs] = hat
        stat[g, at, :] = jnp.broadcast_to(rstd, (ROWS, 128))
        normed[at, :] = (hat * gain).astype(BF16)

    rows_loop(chunk)
    sa[:, gs] = SCALE * dot(up_t[...], normed[...])
    part = dot_t(down[:, gs], normed[...])
    if g == 0:
        down_t[...] = part
    else:
        down_t[...] += part


def project_group(g, wbuf, cot, down, up_row, dn):

    def column(i, carry):
        at = pl.ds(pl.multiple_of(i * 256, 256), 256)
        full = pl.ds(pl.multiple_of(g * GW + i * 256, 256), 256)
        w = wbuf[:, :, :, :, g, :, at].reshape(OUTF, 256)
        dn[:, at] = dot(cot[...], w) + SCALE * dot(up_row[...], down[:, full])
        return carry

    lax.fori_loop(0, GW // 256, column, 0)


def gradient_group(g, z, c, gain_ref, rows_ref, ssd, stat, dn, turned, d, grad):
    gs = slice(g * GW, (g + 1) * GW)
    gain = gain_ref[:, gs]

    def chunk(at):
        hat = ssd[at, gs]
        wg = dn[at, :] * gain
        slope = jnp.mean(hat * wg, axis=-1, keepdims=True)
        d[at, gs] = (stat[g, at, 0:1] * (wg - hat * slope) * silu_of(z, at, gs)).astype(BF16)

    rows_loop(chunk)
    turned[...] = c[:, g * N : (g + 1) * N].astype(F32).T
    low_n = low_lanes(N)

    def body(p):
        dp = d[:, lanes_at(p)]
        halves = []
        for e in (0, 1):
            cw = (turned[...] * jnp.exp(rows_ref[2 * p + e])).astype(BF16)
            halves.append(dot(cw, dp))
        grad[g, p - g * PAIRS] = jnp.where(low_n, halves[0], halves[1]).astype(BF16)

    pairs_loop(g, 2, body)


def backward_group(g, b, c, d, outg, skip_ref, cd_ref, rows_ref, prod, o):
    cs = slice(g * N, (g + 1) * N)
    bg = b[:, cs]
    ri = lax.broadcasted_iota(jnp.int32, (Q, Q), 0)
    ci = lax.broadcasted_iota(jnp.int32, (Q, Q), 1)
    prod[...] = masked(ci >= ri, dot_t(bg, c[:, cs]))
    low = low_lanes(Q)

    def body(p):
        at = lanes_at(p)
        cols = pair_cols(cd_ref, p)
        dp = d[:, at]
        tops, lows = [], []
        for e in (0, 1):
            col = cols[:, e : e + 1]
            row = rows_ref[2 * p + e]
            s00 = (prod[:128, :128] * jnp.exp(jnp.minimum(row[:, :128] - col[:128], 0.0))).astype(BF16)
            s01 = (prod[:128, 128:] * jnp.exp(jnp.minimum(row[:, 128:] - col[:128], 0.0))).astype(BF16)
            s11 = (prod[128:, 128:] * jnp.exp(jnp.minimum(row[:, 128:] - col[128:], 0.0))).astype(BF16)
            tops.append(dot(jnp.concatenate([s00, s01], axis=1), dp))
            lows.append(dot(s11, dp[128:]))
        run = pair_lanes(cols, 0, low)
        cross = jnp.exp(run[Q - 1 : Q] - run) * dot(bg, outg[g, p - g * PAIRS])
        dt = pair_lanes(cols, H, low)
        skip = skip_ref[:, at]
        top = jnp.where(low[:128], tops[0], tops[1]) + cross[:128]
        bottom = jnp.where(low[:128], lows[0], lows[1]) + cross[128:]
        o[:128, at] = (dt[:128] * top + skip * dp[:128].astype(F32)).astype(BF16)
        o[128:, at] = (dt[128:] * bottom + skip * dp[128:].astype(F32)).astype(BF16)

    pairs_loop(g, 2, body)


SLOTS = 350
HALF = RANK // 2
VMEM_SCRATCH = [
    ("wbuf", (4, 4, 4, 2, G, 16, GW), BF16),
    ("x", (Q, INNER), BF16),
    ("z", (Q, INNER), BF16),
    ("b", (Q, G * N), BF16),
    ("c", (Q, G * N), BF16),
    ("cot", (Q, OUTF), BF16),
    ("down", (RANK, INNER), BF16),
    ("up", (RANK, OUTF), BF16),
    ("skip", (1, INNER), F32),
    ("cd", (Q, 128), F32),
    ("rows", (H, 1, Q), F32),
    ("tot", (G, PAIRS, 8, 128), F32),
    ("tots", (8, G, 8, 128), F32),
    ("prod", (Q, Q), F32),
    ("turned", (N, Q), F32),
    ("ssd", (Q, INNER), F32),
    ("stat", (G, Q, 128), F32),
    ("dn", (Q, GW), F32),
    ("normed", (Q, GW), BF16),
    ("d", (Q, INNER), BF16),
    ("up_t", (RANK, Q), BF16),
    ("up_row", (Q, RANK), BF16),
    ("down_t", (RANK, Q), F32),
    ("sa", (RANK, INNER), F32),
    ("sb", (RANK, OUTF), F32),
    ("s_own", (G, PAIRS, N, 128), BF16),
    ("s_got", (8, G, N, 128), BF16),
    ("s_made", (8, G, N, 128), BF16),
    ("s_out", (G, PAIRS, N, 128), BF16),
    ("g_own", (G, PAIRS, N, 128), BF16),
    ("g_got", (8, G, N, 128), BF16),
    ("g_made", (8, G, N, 128), BF16),
    ("g_out", (G, PAIRS, N, 128), BF16),
    ("a0", (HALF, INNER), F32),
    ("b0", (HALF, OUTF), F32),
    ("a0n", (HALF, INNER), BF16),
    ("b0n", (HALF, OUTF), BF16),
    ("a1", (HALF, 1024), F32),
    ("b1", (HALF, 512), F32),
    ("ra1", (3, HALF, 1024), BF16),
    ("rb1", (3, HALF, 512), BF16),
    ("a2", (RANK, 256), F32),
    ("b2", (RANK, 128), F32),
    ("ra2", (3, HALF, 256), F32),
    ("rb2", (3, HALF, 128), F32),
    ("ra3", (3, HALF, 256), F32),
    ("rb3", (3, HALF, 128), F32),
    ("sq", (3, 8, 128), F32),
    ("rsq", (2, 3, 8, 128), F32),
]
SUM_BUFS = (
    "a0", "b0", "a0n", "b0n", "a1", "b1", "ra1", "rb1", "a2", "b2", "ra2", "rb2", "ra3", "rb3", "sq", "rsq",
)
LOADS = ("x", "b", "c", "cot", "up", "z", "down")


def body(*refs):
    names = (
        "dtu", "bias", "alog", "skip_in", "gain", "w", "x", "b", "c", "cot", "up", "z", "down", "o", "da", "db",
    )
    r = dict(zip([n + "_in" if n in LOADS else n for n in names], refs))
    rest = refs[len(names) :]
    r.update(zip([n for n, _, _ in VMEM_SCRATCH], rest))
    send_sem, recv_sem, load_sem, own_sem = rest[len(VMEM_SCRATCH) :]
    place = Place()
    lines = [place.along(axis, step) for axis in "yz" for step in (1, 2, 3)]

    everyone = greet(lines + [{"dp": place.dp, "ctx": place.position(o)} for o in range(1, 8)])
    own = []
    for g in range(G):
        copy = pltpu.make_async_copy(
            r["w"].at[:, pl.ds(g * GW, GW)],
            r["wbuf"].at[place.y, place.z, place.x, place.c, g],
            own_sem.at[g],
        )
        copy.start()
        own.append(copy)
    loads = {}
    for i, name in enumerate(LOADS):
        loads[name] = pltpu.make_async_copy(r[name + "_in"], r[name], load_sem.at[i])
        loads[name].start()
    link = Link(send_sem, recv_sem)
    weight = Weight(place, link, r["wbuf"])
    fwd = Exchange(place, link, r["s_own"], r["tots"], r["s_got"], r["s_made"], r["s_out"], False)
    bwd = Exchange(place, link, r["g_own"], r["tots"], r["g_got"], r["g_made"], r["g_out"], True)
    sums = Sums(place, link, r["sa"], r["sb"], r["da"], r["db"], [r[n] for n in SUM_BUFS]).steps()

    for copy in own:
        copy.wait()
    everyone()
    for g in range(G):
        weight.first(g)
    decay_tables(
        r["dtu"], r["bias"], r["alog"], r["skip_in"], r["cd"], r["rows"], r["tot"], r["skip"]
    )
    me = place.ctx
    totals = []
    for o in range(1, 8):
        k = place.position(o)
        totals.append(link.push(r["tot"].at[:, k], r["tots"].at[me], {"dp": place.dp, "ctx": k}))
    r["tots"][me] = r["tot"][:, me]
    for name in ("x", "b", "c"):
        loads[name].wait()

    def forward(g, half):
        forward_group(
            g, half * PAIRS // 2, (half + 1) * PAIRS // 2, r["x"], r["b"], r["c"], r["skip"], r["cd"], r["rows"],
            r["prod"], r["turned"], r["ssd"], r["s_own"],
        )
        if half:
            fwd.scatter(g)

    def total():
        for copy in totals:
            copy.wait_recv()

    def lora():
        for name in ("cot", "up", "z", "down"):
            loads[name].wait()
        r["up_t"][...] = dot_t(r["up"][...], r["cot"][...]).astype(BF16)
        r["up_row"][...] = dot_t(r["cot"][...], r["up"][...]).astype(BF16)

    def lora_sum():
        r["sb"][...] = SCALE * dot(r["down_t"][...].astype(BF16), r["cot"][...])

    def norm(g):
        fwd.finish(g)
        norm_group(
            g, r["z"], r["c"], r["s_out"], r["gain"], r["cd"], r["ssd"], r["stat"], r["normed"], r["down"],
            r["up_t"], r["down_t"], r["sa"],
        )

    def project(g):
        weight.ready(g)
        project_group(g, r["wbuf"], r["cot"], r["down"], r["up_row"], r["dn"])

    def gradient(g):
        gradient_group(
            g, r["z"], r["c"], r["gain"], r["rows"], r["ssd"], r["stat"], r["dn"], r["turned"], r["d"], r["g_own"]
        )
        bwd.scatter(g)


    def backward(g):
        bwd.finish(g)
        backward_group(
            g, r["b"], r["c"], r["d"], r["g_out"], r["skip"], r["cd"], r["rows"], r["prod"], r["o"]
        )

    forward(0, 0)
    forward(0, 1)
    forward(1, 0)
    weight.jump(0)
    weight.one(1)
    weight.one(2)
    weight.one(3)
    forward(1, 1)
    forward(2, 0)
    forward(2, 1)
    total()
    fwd.combine(0)
    forward(3, 0)
    forward(3, 1)
    weight.two(1)
    weight.last(0)
    lora()
    weight.two(2)
    weight.two(3)
    fwd.combine(1)
    weight.last(1)
    fwd.combine(2)
    norm(0)
    weight.relay(0)
    weight.last(2)
    fwd.combine(3)
    norm(1)
    norm(2)
    weight.relay(1)
    weight.last(3)
    weight.land(0)
    norm(3)
    lora_sum()
    next(sums)
    project(0)
    weight.relay(2)
    weight.land(1)
    gradient(0)
    project(1)
    weight.relay(3)
    next(sums)
    weight.land(2)
    gradient(1)
    bwd.combine(0)
    project(2)
    weight.land(3)
    gradient(2)
    bwd.combine(1)
    project(3)
    next(sums)
    gradient(3)
    bwd.combine(2)
    next(sums)
    backward(0)
    backward(1)
    next(sums)
    bwd.combine(3)
    next(sums)
    backward(2)
    next(sums)
    backward(3)
    next(sums)
    link.drain()


def run_all(dtu, bias, alog, skip, gain, w, x, b, c, cot, up, z, down):
    vmem = pl.BlockSpec(memory_space=pltpu.VMEM)
    hbm = pl.BlockSpec(memory_space=pl.ANY)
    return pl.pallas_call(
        body,
        in_specs=[vmem] * 5 + [hbm] * 8,
        out_specs=[vmem, vmem, vmem],
        out_shape=[
            pltpu.VMEM((Q, INNER), BF16),
            jax.ShapeDtypeStruct((32, RANK), F32),
            jax.ShapeDtypeStruct((16, RANK), F32),
        ],
        scratch_shapes=[pltpu.VMEM(shape, dtype) for _, shape, dtype in VMEM_SCRATCH]
        + [
            pltpu.SemaphoreType.DMA((SLOTS,)),
            pltpu.SemaphoreType.DMA((SLOTS,)),
            pltpu.SemaphoreType.DMA((len(LOADS),)),
            pltpu.SemaphoreType.DMA((G,)),
        ],
        compiler_params=pltpu.CompilerParams(
            collective_id=1, has_side_effects=True, vmem_limit_bytes=VMEM_LIMIT
        ),
        name="whole_step",
    )(dtu, bias, alog, skip, gain, w, x, b, c, cot, up, z, down)


def on_device(x, z, b, c, dtu, bias, alog, skip, gain, down, up, w, cot):
    dx, da, db = run_all(
        dtu.T,
        bias.reshape(1, H),
        alog.reshape(1, H),
        skip.reshape(1, H),
        gain.reshape(1, INNER),
        w,
        x,
        b,
        c,
        cot,
        up,
        z,
        down,
    )
    return dx, da.T, db.T


def solution(mesh):
    rows = P(("dp", "ctx"), None)
    placed = (rows,) * 5 + (P(),) * 6 + (rows, rows)
    return jax.shard_map(
        on_device,
        mesh=mesh,
        in_specs=placed,
        out_specs=(rows, P(None, ("dp", "ctx")), P(None, ("dp", "ctx"))),
        check_vma=False,
    )
```

```python
import jax
import jax.numpy as jnp
from jax import lax
from jax.experimental import pallas as pl
from jax.experimental.pallas import tpu as pltpu
from jax.sharding import PartitionSpec as P

H = 64
P_SIZE = 64
N = 128
G = 4
Q = 256
INNER = 4096
OUTF = 2048
RANK = 64
GW = INNER // G
HG = H // G
PAIRS = HG // 2
EPS_NORM = 1e-05
CLIP_EPSILON = 1e-06
SCALE = 2.0
MESH = pl.DeviceIdType.MESH
F32 = jnp.float32
BF16 = jnp.bfloat16
VMEM_LIMIT = 56 * 1024 * 1024


def dot(a, b):
    return lax.dot_general(a, b, (((1,), (0,)), ((), ())), preferred_element_type=F32)


def dot_t(a, b):
    return lax.dot_general(a, b, (((1,), (1,)), ((), ())), preferred_element_type=F32)


def low_lanes(rows):
    return lax.broadcasted_iota(jnp.int32, (rows, 128), 1) < 64


def pair_cols(cd_ref, p):
    return pltpu.roll(cd_ref[...], lax.rem(128 - 2 * p, 128), 1)


def pair_lanes(cols, at, low):
    return jnp.where(low, cols[:, at : at + 1], cols[:, at + 1 : at + 2])


def lanes_at(p):
    return pl.ds(pl.multiple_of(p * 128, 128), 128)


class Place:
    def __init__(self):
        self.dp = lax.axis_index("dp")
        self.ctx = lax.axis_index("ctx")
        self.y = lax.div(self.dp, 4)
        self.z = lax.rem(self.dp, 4)
        self.x = lax.div(self.ctx, 2)
        self.c = lax.rem(self.ctx, 2)

    def coord(self, axis):
        return {"x": self.x, "y": self.y, "z": self.z}[axis]

    def along(self, axis, step):
        if axis == "x":
            return {"dp": self.dp, "ctx": lax.rem(self.x + step, 4) * 2 + self.c}
        if axis == "y":
            return {"dp": lax.rem(self.y + step, 4) * 4 + self.z, "ctx": self.ctx}
        return {"dp": self.y * 4 + lax.rem(self.z + step, 4), "ctx": self.ctx}

    def partner(self):
        return {"dp": self.dp, "ctx": self.x * 2 + 1 - self.c}

    def position(self, step):
        return lax.rem(self.ctx + step, 8)


def greet(devices):
    barrier = pltpu.get_barrier_semaphore()
    for device in devices:
        pl.semaphore_signal(barrier, inc=1, device_id=device, device_id_type=MESH)
    return lambda: pl.semaphore_wait(barrier, len(devices))


class Link:
    def __init__(self, send_sem, recv_sem):
        self.send_sem, self.recv_sem, self.used, self.sent = send_sem, recv_sem, 0, []

    def push(self, src, dst, device):
        copy = pltpu.make_async_remote_copy(
            src_ref=src,
            dst_ref=dst,
            send_sem=self.send_sem.at[self.used],
            recv_sem=self.recv_sem.at[self.used],
            device_id=device,
            device_id_type=MESH,
        )
        self.used += 1
        copy.start()
        self.sent.append(copy)
        return copy

    def settle(self, copies):
        for copy in copies:
            copy.wait_send()
        self.sent = [old for old in self.sent if all(old is not copy for copy in copies)]

    def drain(self):
        for copy in self.sent:
            copy.wait_send()


class Exchange:
    def __init__(self, place, link, own, tots, got, made, out, reverse):
        self.place, self.link, self.own, self.tots = place, link, own, tots
        self.got, self.made, self.out, self.reverse = got, made, out, reverse
        self.first, self.second = {}, {}

    def peer(self, k):
        return {"dp": self.place.dp, "ctx": k}

    def scatter(self, g):
        me = self.place.ctx
        self.first[g] = []
        for o in range(1, 8):
            k = self.place.position(o)
            self.first[g].append(self.link.push(self.own.at[g, k], self.got.at[me, g], self.peer(k)))
        self.got[me, g] = self.own[g, me]

    def combine(self, g):
        for copy in self.first[g]:
            copy.wait_recv()
        run = jnp.zeros((N, 128), F32)
        for j in range(7, -1, -1) if self.reverse else range(8):
            self.made[j, g] = run.astype(BF16)
            run = jnp.exp(self.tots[j, g, 0:1]) * run + self.got[j, g].astype(F32)
        me = self.place.ctx
        self.second[g] = []
        for o in range(1, 8):
            j = self.place.position(o)
            self.second[g].append(self.link.push(self.made.at[j, g], self.out.at[g, me], self.peer(j)))
        self.out[g, me] = self.made[me, g]

    def finish(self, g):
        for copy in self.second[g]:
            copy.wait_recv()


ORDERS = (("x", "y", "z"), ("y", "z", "x"), ("x", "z", "y"))
TILES = ((4, 1, 3), (3, 1, 4), (3, 2, 3), (3, 2, 3))


class Part:
    def __init__(self, place, link, buf, index):
        self.place, self.link, self.buf = place, link, buf
        self.order = ORDERS[index]
        self.start = [sum(tiles[:index]) for tiles in TILES]
        self.tiles = [tiles[index] for tiles in TILES]
        self.near, self.far = {}, {}

    def view(self, stage, step, g, tiles=None):
        picks = {}
        for i, axis in enumerate(self.order):
            if i < stage:
                picks[axis] = slice(None)
            elif i == stage:
                picks[axis] = lax.rem(self.place.coord(axis) + step, 4)
            else:
                picks[axis] = self.place.coord(axis)
        lo, count = (0, self.tiles[g]) if tiles is None else tiles
        return self.buf.at[
            picks["y"],
            picks["z"],
            picks["x"],
            self.place.c,
            g,
            slice(None),
            pl.ds((self.start[g] + lo) * 128, count * 128),
        ]

    def push(self, view, device):
        return self.link.push(view, view, device)

    def direct(self, stage, g):
        axis = self.order[stage]
        view = self.view(stage, 0, g)
        self.far[stage, g] = [self.push(view, self.place.along(axis, o)) for o in (1, 3, 2)]

    def hop_one(self, stage, g):
        axis = self.order[stage]
        view = self.view(stage, 0, g)
        self.near[stage, g] = (
            self.push(view, self.place.along(axis, 1)),
            self.push(view, self.place.along(axis, 3)),
        )

    def hop_two(self, stage, g):
        axis = self.order[stage]
        count = self.tiles[g]
        lo = (count + 1 - g % 2) // 2
        left, right = self.near[stage, g]
        self.far[stage, g] = []
        left.wait_recv()
        if lo:
            self.far[stage, g].append(self.push(self.view(stage, 3, g, (0, lo)), self.place.along(axis, 1)))
        right.wait_recv()
        if lo < count:
            self.far[stage, g].append(
                self.push(self.view(stage, 1, g, (lo, count - lo)), self.place.along(axis, 3))
            )

    def arrive(self, stage, g):
        for copy in self.far[stage, g]:
            copy.wait_recv()

    def share(self, step, g):
        return self.push(self.view(2, step, g), self.place.partner())


class Weight:
    def __init__(self, place, link, buf):
        self.parts = [Part(place, link, buf, i) for i in range(3)]
        self.shared = {g: [] for g in range(G)}

    def first(self, g):
        for part in self.parts:
            part.direct(0, g)

    def jump(self, g):
        for part in self.parts:
            part.arrive(0, g)
            part.direct(1, g)

    def one(self, g):
        for part in self.parts:
            part.arrive(0, g)
            part.hop_one(1, g)

    def two(self, g):
        for part in self.parts:
            part.hop_two(1, g)

    def last(self, g):
        for part in self.parts:
            part.arrive(1, g)
            part.hop_one(2, g)
        for part in self.parts:
            self.shared[g].append(part.share(0, g))

    def relay(self, g):
        for part in self.parts:
            part.hop_two(2, g)
        for part in self.parts:
            self.shared[g].append(part.share(3, g))
            self.shared[g].append(part.share(1, g))

    def land(self, g):
        for part in self.parts:
            part.arrive(2, g)
            self.shared[g].append(part.share(2, g))

    def ready(self, g):
        for copy in self.shared[g]:
            copy.wait_recv()


class Sums:
    def __init__(self, place, link, sa, sb, da, db, bufs):
        self.place, self.link, self.sa, self.sb, self.da, self.db = place, link, sa, sb, da, db
        self.bufs = bufs

    def spread(self, axis, wide, narrow, a, b, ra, rb):
        copies = []
        for o in (1, 2, 3):
            to = lax.rem(self.place.coord(axis) + o, 4)
            device = self.place.along(axis, o)
            ca = pl.ds(pl.multiple_of(to * wide, 128), wide)
            cb = pl.ds(pl.multiple_of(to * narrow, 128), narrow)
            copies.append(self.link.push(a.at[:, ca], ra.at[o - 1], device))
            copies.append(self.link.push(b.at[:, cb], rb.at[o - 1], device))
        return copies

    def summed(self, axis, wide, narrow, a, b, ra, rb):
        own = self.place.coord(axis)
        ca = pl.ds(pl.multiple_of(own * wide, 128), wide)
        cb = pl.ds(pl.multiple_of(own * narrow, 128), narrow)
        return (
            a[:, ca] + (ra[0].astype(F32) + ra[1].astype(F32) + ra[2].astype(F32)),
            b[:, cb] + (rb[0].astype(F32) + rb[1].astype(F32) + rb[2].astype(F32)),
        )

    def steps(self):
        place, push = self.place, self.link.push
        a0, b0, a0n, b0n, a1, b1, ra1, rb1, a2, b2, ra2, rb2, ra3, rb3, sq, rsq = self.bufs
        half = RANK // 2
        mine = pl.ds(pl.multiple_of(place.c * half, half), half)
        theirs = pl.ds(pl.multiple_of((1 - place.c) * half, half), half)
        partner = place.partner()

        def arrived(copies):
            for copy in copies:
                copy.wait_recv()

        copies = [push(self.sa.at[theirs], a0, partner), push(self.sb.at[theirs], b0, partner)]
        yield
        arrived(copies)
        a0[...] += self.sa[mine]
        b0[...] += self.sb[mine]
        a0n[...] = a0[...].astype(BF16)
        b0n[...] = b0[...].astype(BF16)
        copies = self.spread("y", 1024, 512, a0n, b0n, ra1, rb1)
        yield
        arrived(copies)
        a1[...], b1[...] = self.summed("y", 1024, 512, a0, b0, ra1, rb1)
        copies = self.spread("z", 256, 128, a1, b1, ra2, rb2)
        yield
        arrived(copies)
        a2[mine], b2[mine] = self.summed("z", 256, 128, a1, b1, ra2, rb2)
        copies = []
        for o in (1, 2, 3):
            device = place.along("x", o)
            copies.append(push(a2.at[mine], ra3.at[o - 1], device))
            copies.append(push(b2.at[mine], rb3.at[o - 1], device))
        yield
        arrived(copies)
        self.link.settle(copies)
        a2[mine] += ra3[0] + ra3[1] + ra3[2]
        b2[mine] += rb3[0] + rb3[1] + rb3[2]
        copies = [push(a2.at[mine], a2.at[mine], partner), push(b2.at[mine], b2.at[mine], partner)]
        yield
        arrived(copies)
        a = a2[...]
        b = b2[...]
        row = lax.broadcasted_iota(jnp.int32, (8, 128), 0)
        sq[0] = jnp.where(row == 0, jnp.sum(a * a), jnp.sum(b * b))
        for i, axis in enumerate("yz"):
            copies = [push(sq.at[i], rsq.at[i, o - 1], place.along(axis, o)) for o in (1, 2, 3)]
            yield
            arrived(copies)
            sq[i + 1] = sq[i] + (rsq[i, 0] + rsq[i, 1] + rsq[i, 2])
        total = sq[2]
        root_a = jnp.sqrt(total[0:1, 0:1] / (RANK * INNER) + CLIP_EPSILON)
        root_b = jnp.sqrt(total[1:2, 0:1] / (RANK * OUTF) + CLIP_EPSILON)
        a = jnp.where(place.ctx >= 4, a2[:, 128:], a2[:, :128]) / jnp.maximum(1.0, root_a)
        b = b2[...] / jnp.maximum(1.0, root_b)
        a = pltpu.roll(a, lax.rem(256 - 32 * place.ctx, 128), 1)
        b = pltpu.roll(b, lax.rem(128 - 16 * place.ctx, 128), 1)
        self.da[...] = a.T[:32, :]
        self.db[...] = b.T[:16, :]
        yield


def decay_tables(dtu_ref, bias_ref, alog_ref, skip_in, cd_ref, rows_ref, tot_ref, skip_ref):
    step = jax.nn.softplus(dtu_ref[...].T + bias_ref[...])
    run = -jnp.exp(alog_ref[...]) * step
    rows = lax.broadcasted_iota(jnp.int32, (Q, H), 0)
    shift = 1
    while shift < Q:
        run = run + jnp.where(rows >= shift, pltpu.roll(run, shift, 0), 0.0)
        shift *= 2
    both = jnp.concatenate([run, step], axis=1)
    cd_ref[...] = both
    turned = both.T
    for h in range(H):
        rows_ref[h] = turned[h : h + 1, :]
    low = low_lanes(8)
    last = both[Q - 1 : Q, :]
    for p in range(H // 2):
        pair = jnp.where(low, last[:, 2 * p : 2 * p + 1], last[:, 2 * p + 1 : 2 * p + 2])
        tot_ref[p // PAIRS, p % PAIRS] = pair
        skip = skip_in[...]
        skip_ref[:, p * 128 : (p + 1) * 128] = jnp.where(
            low[:1], skip[:, 2 * p : 2 * p + 1], skip[:, 2 * p + 1 : 2 * p + 2]
        )


def masked(keep, tile):
    return jnp.where(keep, tile, 0.0)


def pairs_loop(g, width, body, first=0, last=PAIRS):
    def step(i, carry):
        for u in range(width):
            body(g * PAIRS + i * width + u)
        return carry

    lax.fori_loop(first // width, last // width, step, 0)


def forward_group(g, first, last, x, b, c, skip_ref, cd_ref, rows_ref, prod, turned, ssd, s_ref):
    cs = slice(g * N, (g + 1) * N)
    bg = b[:, cs]
    if first == 0:
        turned[...] = bg.astype(F32).T
        ri = lax.broadcasted_iota(jnp.int32, (Q, Q), 0)
        ci = lax.broadcasted_iota(jnp.int32, (Q, Q), 1)
        prod[...] = masked(ri >= ci, dot_t(c[:, cs], bg))
    low = low_lanes(Q)

    def body(p):
        at = lanes_at(p)
        cols = pair_cols(cd_ref, p)
        xp = x[:, at].astype(F32)
        xdt = (xp * pair_lanes(cols, H, low)).astype(BF16)
        tops, lows, states = [], [], []
        for e in (0, 1):
            col = cols[:, e : e + 1]
            row = rows_ref[2 * p + e]
            s00 = (prod[:128, :128] * jnp.exp(jnp.minimum(col[:128] - row[:, :128], 0.0))).astype(BF16)
            s10 = (prod[128:, :128] * jnp.exp(jnp.minimum(col[128:] - row[:, :128], 0.0))).astype(BF16)
            s11 = (prod[128:, 128:] * jnp.exp(jnp.minimum(col[128:] - row[:, 128:], 0.0))).astype(BF16)
            tops.append(dot(s00, xdt[:128]))
            lows.append(dot(jnp.concatenate([s10, s11], axis=1), xdt))
            bw = (turned[...] * jnp.exp(row[:, Q - 1 : Q] - row)).astype(BF16)
            states.append(dot(bw, xdt))
        skip = skip_ref[:, at]
        ssd[:128, at] = jnp.where(low[:128], tops[0], tops[1]) + skip * xp[:128]
        ssd[128:, at] = jnp.where(low[:128], lows[0], lows[1]) + skip * xp[128:]
        s_ref[g, p - g * PAIRS] = jnp.where(low[:N], states[0], states[1]).astype(BF16)

    pairs_loop(g, 2, body, first, last)


ROWS = 64


def rows_loop(body):
    def step(i, carry):
        body(pl.ds(pl.multiple_of(i * ROWS, ROWS), ROWS))
        return carry

    lax.fori_loop(0, Q // ROWS, step, 0)


def silu_of(z, at, gs):
    zf = z[at, gs].astype(F32)
    return 0.5 * zf * (1.0 + jnp.tanh(0.5 * zf))


def norm_group(g, z, c, inc, gain_ref, cd_ref, ssd, stat, normed, down, up_t, down_t, sa):
    gs = slice(g * GW, (g + 1) * GW)
    cg = c[:, g * N : (g + 1) * N]
    low = low_lanes(Q)

    def inter(p):
        at = lanes_at(p)
        cols = pair_cols(cd_ref, p)
        ssd[:, at] += jnp.exp(pair_lanes(cols, 0, low)) * dot(cg, inc[g, p - g * PAIRS])

    pairs_loop(g, 2, inter)
    gain = gain_ref[:, gs]

    def chunk(at):
        gated = ssd[at, gs] * silu_of(z, at, gs)
        rstd = lax.rsqrt(jnp.mean(gated * gated, axis=-1, keepdims=True) + EPS_NORM)
        hat = gated * rstd
        ssd[at, gs] = hat
        stat[g, at, :] = jnp.broadcast_to(rstd, (ROWS, 128))
        normed[at, :] = (hat * gain).astype(BF16)

    rows_loop(chunk)
    sa[:, gs] = SCALE * dot(up_t[...], normed[...])
    part = dot_t(down[:, gs], normed[...])
    if g == 0:
        down_t[...] = part
    else:
        down_t[...] += part


def project_group(g, wbuf, cot, down, up_row, dn):

    def column(i, carry):
        at = pl.ds(pl.multiple_of(i * 256, 256), 256)
        full = pl.ds(pl.multiple_of(g * GW + i * 256, 256), 256)
        w = wbuf[:, :, :, :, g, :, at].reshape(OUTF, 256)
        dn[:, at] = dot(cot[...], w) + SCALE * dot(up_row[...], down[:, full])
        return carry

    lax.fori_loop(0, GW // 256, column, 0)


def gradient_group(g, z, c, gain_ref, rows_ref, ssd, stat, dn, turned, d, grad):
    gs = slice(g * GW, (g + 1) * GW)
    gain = gain_ref[:, gs]

    def chunk(at):
        hat = ssd[at, gs]
        wg = dn[at, :] * gain
        slope = jnp.mean(hat * wg, axis=-1, keepdims=True)
        d[at, gs] = (stat[g, at, 0:1] * (wg - hat * slope) * silu_of(z, at, gs)).astype(BF16)

    rows_loop(chunk)
    turned[...] = c[:, g * N : (g + 1) * N].astype(F32).T
    low_n = low_lanes(N)

    def body(p):
        dp = d[:, lanes_at(p)]
        halves = []
        for e in (0, 1):
            cw = (turned[...] * jnp.exp(rows_ref[2 * p + e])).astype(BF16)
            halves.append(dot(cw, dp))
        grad[g, p - g * PAIRS] = jnp.where(low_n, halves[0], halves[1]).astype(BF16)

    pairs_loop(g, 2, body)


def backward_group(g, b, c, d, outg, skip_ref, cd_ref, rows_ref, prod, o):
    cs = slice(g * N, (g + 1) * N)
    bg = b[:, cs]
    ri = lax.broadcasted_iota(jnp.int32, (Q, Q), 0)
    ci = lax.broadcasted_iota(jnp.int32, (Q, Q), 1)
    prod[...] = masked(ci >= ri, dot_t(bg, c[:, cs]))
    low = low_lanes(Q)

    def body(p):
        at = lanes_at(p)
        cols = pair_cols(cd_ref, p)
        dp = d[:, at]
        tops, lows = [], []
        for e in (0, 1):
            col = cols[:, e : e + 1]
            row = rows_ref[2 * p + e]
            s00 = (prod[:128, :128] * jnp.exp(jnp.minimum(row[:, :128] - col[:128], 0.0))).astype(BF16)
            s01 = (prod[:128, 128:] * jnp.exp(jnp.minimum(row[:, 128:] - col[:128], 0.0))).astype(BF16)
            s11 = (prod[128:, 128:] * jnp.exp(jnp.minimum(row[:, 128:] - col[128:], 0.0))).astype(BF16)
            tops.append(dot(jnp.concatenate([s00, s01], axis=1), dp))
            lows.append(dot(s11, dp[128:]))
        run = pair_lanes(cols, 0, low)
        cross = jnp.exp(run[Q - 1 : Q] - run) * dot(bg, outg[g, p - g * PAIRS])
        dt = pair_lanes(cols, H, low)
        skip = skip_ref[:, at]
        top = jnp.where(low[:128], tops[0], tops[1]) + cross[:128]
        bottom = jnp.where(low[:128], lows[0], lows[1]) + cross[128:]
        o[:128, at] = (dt[:128] * top + skip * dp[:128].astype(F32)).astype(BF16)
        o[128:, at] = (dt[128:] * bottom + skip * dp[128:].astype(F32)).astype(BF16)

    pairs_loop(g, 2, body)


SLOTS = 350
HALF = RANK // 2
VMEM_SCRATCH = [
    ("wbuf", (4, 4, 4, 2, G, 16, GW), BF16),
    ("x", (Q, INNER), BF16),
    ("z", (Q, INNER), BF16),
    ("b", (Q, G * N), BF16),
    ("c", (Q, G * N), BF16),
    ("cot", (Q, OUTF), BF16),
    ("down", (RANK, INNER), BF16),
    ("up", (RANK, OUTF), BF16),
    ("skip", (1, INNER), F32),
    ("cd", (Q, 128), F32),
    ("rows", (H, 1, Q), F32),
    ("tot", (G, PAIRS, 8, 128), F32),
    ("tots", (8, G, 8, 128), F32),
    ("prod", (Q, Q), F32),
    ("turned", (N, Q), F32),
    ("ssd", (Q, INNER), F32),
    ("stat", (G, Q, 128), F32),
    ("dn", (Q, GW), F32),
    ("normed", (Q, GW), BF16),
    ("d", (Q, INNER), BF16),
    ("up_t", (RANK, Q), BF16),
    ("up_row", (Q, RANK), BF16),
    ("down_t", (RANK, Q), F32),
    ("sa", (RANK, INNER), F32),
    ("sb", (RANK, OUTF), F32),
    ("s_own", (G, PAIRS, N, 128), BF16),
    ("s_got", (8, G, N, 128), BF16),
    ("s_made", (8, G, N, 128), BF16),
    ("s_out", (G, PAIRS, N, 128), BF16),
    ("g_own", (G, PAIRS, N, 128), BF16),
    ("g_got", (8, G, N, 128), BF16),
    ("g_made", (8, G, N, 128), BF16),
    ("g_out", (G, PAIRS, N, 128), BF16),
    ("a0", (HALF, INNER), F32),
    ("b0", (HALF, OUTF), F32),
    ("a0n", (HALF, INNER), BF16),
    ("b0n", (HALF, OUTF), BF16),
    ("a1", (HALF, 1024), F32),
    ("b1", (HALF, 512), F32),
    ("ra1", (3, HALF, 1024), BF16),
    ("rb1", (3, HALF, 512), BF16),
    ("a2", (RANK, 256), F32),
    ("b2", (RANK, 128), F32),
    ("ra2", (3, HALF, 256), F32),
    ("rb2", (3, HALF, 128), F32),
    ("ra3", (3, HALF, 256), F32),
    ("rb3", (3, HALF, 128), F32),
    ("sq", (3, 8, 128), F32),
    ("rsq", (2, 3, 8, 128), F32),
]
SUM_BUFS = (
    "a0", "b0", "a0n", "b0n", "a1", "b1", "ra1", "rb1", "a2", "b2", "ra2", "rb2", "ra3", "rb3", "sq", "rsq",
)
LOADS = ("x", "b", "c", "cot", "up", "z", "down")


def body(*refs):
    names = (
        "dtu", "bias", "alog", "skip_in", "gain", "w", "x", "b", "c", "cot", "up", "z", "down", "o", "da", "db",
    )
    r = dict(zip([n + "_in" if n in LOADS else n for n in names], refs))
    rest = refs[len(names) :]
    r.update(zip([n for n, _, _ in VMEM_SCRATCH], rest))
    send_sem, recv_sem, load_sem, own_sem = rest[len(VMEM_SCRATCH) :]
    place = Place()
    lines = [place.along(axis, step) for axis in "yz" for step in (1, 2, 3)]

    everyone = greet(lines + [{"dp": place.dp, "ctx": place.position(o)} for o in range(1, 8)])
    own = []
    for g in range(G):
        copy = pltpu.make_async_copy(
            r["w"].at[:, pl.ds(g * GW, GW)],
            r["wbuf"].at[place.y, place.z, place.x, place.c, g],
            own_sem.at[g],
        )
        copy.start()
        own.append(copy)
    loads = {}
    for i, name in enumerate(LOADS):
        loads[name] = pltpu.make_async_copy(r[name + "_in"], r[name], load_sem.at[i])
        loads[name].start()
    link = Link(send_sem, recv_sem)
    weight = Weight(place, link, r["wbuf"])
    fwd = Exchange(place, link, r["s_own"], r["tots"], r["s_got"], r["s_made"], r["s_out"], False)
    bwd = Exchange(place, link, r["g_own"], r["tots"], r["g_got"], r["g_made"], r["g_out"], True)
    sums = Sums(place, link, r["sa"], r["sb"], r["da"], r["db"], [r[n] for n in SUM_BUFS]).steps()

    for copy in own:
        copy.wait()
    everyone()
    for g in range(G):
        weight.first(g)
    decay_tables(
        r["dtu"], r["bias"], r["alog"], r["skip_in"], r["cd"], r["rows"], r["tot"], r["skip"]
    )
    me = place.ctx
    totals = []
    for o in range(1, 8):
        k = place.position(o)
        totals.append(link.push(r["tot"].at[:, k], r["tots"].at[me], {"dp": place.dp, "ctx": k}))
    r["tots"][me] = r["tot"][:, me]
    for name in ("x", "b", "c"):
        loads[name].wait()

    def forward(g, half):
        forward_group(
            g, half * PAIRS // 2, (half + 1) * PAIRS // 2, r["x"], r["b"], r["c"], r["skip"], r["cd"], r["rows"],
            r["prod"], r["turned"], r["ssd"], r["s_own"],
        )
        if half:
            fwd.scatter(g)

    def total():
        for copy in totals:
            copy.wait_recv()

    def lora():
        for name in ("cot", "up", "z", "down"):
            loads[name].wait()
        r["up_t"][...] = dot_t(r["up"][...], r["cot"][...]).astype(BF16)
        r["up_row"][...] = dot_t(r["cot"][...], r["up"][...]).astype(BF16)

    def lora_sum():
        r["sb"][...] = SCALE * dot(r["down_t"][...].astype(BF16), r["cot"][...])

    def norm(g):
        fwd.finish(g)
        norm_group(
            g, r["z"], r["c"], r["s_out"], r["gain"], r["cd"], r["ssd"], r["stat"], r["normed"], r["down"],
            r["up_t"], r["down_t"], r["sa"],
        )

    def project(g):
        weight.ready(g)
        project_group(g, r["wbuf"], r["cot"], r["down"], r["up_row"], r["dn"])

    def gradient(g):
        gradient_group(
            g, r["z"], r["c"], r["gain"], r["rows"], r["ssd"], r["stat"], r["dn"], r["turned"], r["d"], r["g_own"]
        )
        bwd.scatter(g)


    def backward(g):
        bwd.finish(g)
        backward_group(
            g, r["b"], r["c"], r["d"], r["g_out"], r["skip"], r["cd"], r["rows"], r["prod"], r["o"]
        )

    forward(0, 0)
    forward(0, 1)
    forward(1, 0)
    weight.jump(0)
    weight.one(1)
    weight.one(2)
    weight.one(3)
    forward(1, 1)
    forward(2, 0)
    forward(2, 1)
    total()
    fwd.combine(0)
    forward(3, 0)
    forward(3, 1)
    weight.two(1)
    weight.last(0)
    lora()
    weight.two(2)
    weight.two(3)
    fwd.combine(1)
    weight.last(1)
    fwd.combine(2)
    norm(0)
    weight.relay(0)
    weight.last(2)
    fwd.combine(3)
    norm(1)
    norm(2)
    weight.relay(1)
    weight.last(3)
    weight.land(0)
    norm(3)
    lora_sum()
    next(sums)
    project(0)
    weight.relay(2)
    weight.land(1)
    gradient(0)
    project(1)
    weight.relay(3)
    next(sums)
    weight.land(2)
    gradient(1)
    bwd.combine(0)
    project(2)
    weight.land(3)
    gradient(2)
    bwd.combine(1)
    project(3)
    next(sums)
    gradient(3)
    next(sums)
    bwd.combine(2)
    backward(0)
    backward(1)
    bwd.combine(3)
    next(sums)
    backward(2)
    next(sums)
    next(sums)
    backward(3)
    next(sums)
    link.drain()


def run_all(dtu, bias, alog, skip, gain, w, x, b, c, cot, up, z, down):
    vmem = pl.BlockSpec(memory_space=pltpu.VMEM)
    hbm = pl.BlockSpec(memory_space=pl.ANY)
    return pl.pallas_call(
        body,
        in_specs=[vmem] * 5 + [hbm] * 8,
        out_specs=[vmem, vmem, vmem],
        out_shape=[
            pltpu.VMEM((Q, INNER), BF16),
            jax.ShapeDtypeStruct((32, RANK), F32),
            jax.ShapeDtypeStruct((16, RANK), F32),
        ],
        scratch_shapes=[pltpu.VMEM(shape, dtype) for _, shape, dtype in VMEM_SCRATCH]
        + [
            pltpu.SemaphoreType.DMA((SLOTS,)),
            pltpu.SemaphoreType.DMA((SLOTS,)),
            pltpu.SemaphoreType.DMA((len(LOADS),)),
            pltpu.SemaphoreType.DMA((G,)),
        ],
        compiler_params=pltpu.CompilerParams(
            collective_id=1, has_side_effects=True, vmem_limit_bytes=VMEM_LIMIT
        ),
        name="whole_step",
    )(dtu, bias, alog, skip, gain, w, x, b, c, cot, up, z, down)


def on_device(x, z, b, c, dtu, bias, alog, skip, gain, down, up, w, cot):
    dx, da, db = run_all(
        dtu.T,
        bias.reshape(1, H),
        alog.reshape(1, H),
        skip.reshape(1, H),
        gain.reshape(1, INNER),
        w,
        x,
        b,
        c,
        cot,
        up,
        z,
        down,
    )
    return dx, da.T, db.T


def solution(mesh):
    rows = P(("dp", "ctx"), None)
    placed = (rows,) * 5 + (P(),) * 6 + (rows, rows)
    return jax.shard_map(
        on_device,
        mesh=mesh,
        in_specs=placed,
        out_specs=(rows, P(None, ("dp", "ctx")), P(None, ("dp", "ctx"))),
        check_vma=False,
    )
```
